32 devices in a mesh: dom: 16 (over z, y, x), col: 2 (over core).
Axes of the slice: x: 2, y: 2, z: 4, core: 2. Of those that a mesh axis runs over, the one named last changes fastest.
Arguments:
- diag_blocks: bfloat16 [3072, 128, 128], P(('dom', 'col')), may hold values from -0.375 to 0.375
- couplings: bfloat16 [3072, 6, 128], P(('dom', 'col')), may hold values from -1.1953125 to 1.1953125
- columns: int32 [3072, 6], P(('dom', 'col')), may hold values from 0 to 119, as said below
- send_rows: int32 [32, 24], P(('dom', 'col')), may hold values from 0 to 95
- shifts: float32 [6], replicated, may hold values from -0.5 to 0.5
- start_vector: float32 [3072, 128], P(('dom', 'col')), may hold values from -30 to 30
- sketch: bfloat16 [32, 3072, 128], P(None, ('dom', 'col')), may hold values from -0.0017089844 to 0.0017089844
Outputs:
- orthonormal: float32 [7, 3072, 128], P(None, ('dom', 'col'))
- factor: float32 [7, 7], replicated
- sketch_factor: float32 [7, 7], replicated
The draws below stay inside these ranges and needn't reach their ends.
Inputs may be any that keep to these rules, and one draw needn't show every extreme that they name: `columns`: each device's column indices point into its extended vector: its 96 own row blocks, then 4 blocks from the lower col neighbour, 4 from the upper one, then 4 from the dom partner of each bisection level, lowest level first. Every received position is read by some block row of the device. `send_rows`: per device: the first 4 entries go to the lower col neighbour, the next 4 to the upper one, then 4 to the dom partner of each level, lowest level first.
All inputs are finite; a program needn't handle non-finite values.
Results may differ from the reference program's by a relative error of at most 0.0003.
Values sent between devices are 32-bit elements; how exact they have to be, the bound alone decides.
No kernel may reach another device: no remote copies, remote signals or barrier semaphores. Data moves between devices by JAX's collectives and lax.ppermute only.
A program may use at most 64 MiB of HBM per device.

```python
import math
import jax
import jax.numpy as jnp
from jax import lax

BS = 128
RB = 96
NEIGH = 6
S = 6
SKETCH = 32
FACE = 4
LEVELS = 4
HALO = 24
VECS = 7
BLOCKS = 3072
ROWS = 393216
N_DOM = 16
N_COL = 2


def draw_columns(key, part):
    device_total = BLOCKS // RB
    slot_count = RB * NEIGH

    def one_device(device_key):
        first_key, second_key = jax.random.split(device_key)
        chosen = jax.random.randint(first_key, (slot_count,), 0, RB + HALO, dtype=jnp.int32)
        shuffled = jax.random.permutation(second_key, slot_count)
        chosen = chosen.at[shuffled[:HALO]].set(RB + jnp.arange(HALO, dtype=jnp.int32))
        chosen = chosen.at[shuffled[HALO]].set(0)
        return chosen.reshape(RB, NEIGH)
    device_keys = jax.random.split(jax.random.fold_in(key, 7), device_total)
    return jax.vmap(one_device)(device_keys).reshape(BLOCKS, NEIGH).astype(jnp.int32)


def draw_start_vector(key, part):
    scale_key, value_key = jax.random.split(jax.random.fold_in(key, 11))
    device_total = BLOCKS // RB
    device_place = (jnp.arange(BLOCKS, dtype=jnp.int32) // RB).astype(jnp.float32)
    device_ramp = jnp.exp(device_place * (math.log(3.0) / max(device_total - 1, 1)))
    scales = jnp.exp(jax.random.uniform(scale_key, (BLOCKS, BS), jnp.float32) * math.log(10.0))
    values = jnp.clip(jax.random.normal(value_key, (BLOCKS, BS), jnp.float32), -4.0, 4.0)
    return values * scales * device_ramp[:, None] * 0.25


def plant(entries, stream_key, low, high):
    shape = entries.shape
    spot = [jax.random.randint(jax.random.fold_in(stream_key, axis), (), 0, shape[axis]) for axis in range(len(shape))]
    entries = entries.at[tuple(spot)].set(low)
    longest = shape.index(max(shape))
    spot[longest] = (spot[longest] + 1) % shape[longest]
    return entries.at[tuple(spot)].set(high)


def level_of(key, extent, cuts, low, top_value):
    factor_of = 1.0
    for position, parts in cuts:
        heights = jax.random.uniform(jax.random.fold_in(jax.random.fold_in(key, 6), position), (parts,), jnp.float32, low / len(cuts), top_value / len(cuts))
        factor_of = factor_of * jnp.repeat(jnp.exp(heights), extent[position] // parts).reshape((-1,) + (1,) * (len(extent) - 1 - position))
    return factor_of


def gaussian(stream_key, dims, scale, reach, cuts=(), kind=jnp.bfloat16):
    drawn = scale * jax.random.normal(stream_key, dims, jnp.float32)
    if cuts:
        drawn = drawn * level_of(stream_key, dims, cuts, -0.22, 0.18)
    return jnp.clip(drawn, -reach, reach).astype(kind)


def setup_inputs(seed: int = 0) -> dict:
    arg_keys = jax.random.split(jax.random.key(seed), 8)
    return {
        "diag_blocks": gaussian(arg_keys[0], (BLOCKS, BS, BS), (2 * BS) ** -0.5, 0.375, ((0, 32),)),
        "couplings": gaussian(arg_keys[1], (BLOCKS, NEIGH, BS), 0.29, 1.1953125, ((0, 32),)),
        "columns": draw_columns(jax.random.fold_in(arg_keys[7], 71), 0),
        "send_rows": plant(jax.random.randint(arg_keys[3], (BLOCKS // RB, HALO), 0, RB), jax.random.fold_in(arg_keys[3], 1), 0, RB - 1).astype(jnp.int32),
        "shifts": jnp.clip(jax.random.uniform(arg_keys[4], (S,), jnp.float32, -0.5, 0.5), -0.5, 0.5),
        "start_vector": draw_start_vector(jax.random.fold_in(arg_keys[7], 71), 0),
        "sketch": gaussian(arg_keys[6], (SKETCH, BLOCKS, BS), (SKETCH * ROWS) ** -0.5, 0.0017089844, ((1, 32),)),
    }


highest = lax.Precision.HIGHEST

def cholesky_upper(gram_matrix):
    order_size = gram_matrix.shape[0]
    zero_entry = jnp.zeros((), gram_matrix.dtype)
    upper = [[zero_entry for col_index in range(order_size)] for row_index in range(order_size)]
    for pivot in range(order_size):
        diag_value = gram_matrix[pivot, pivot]
        for inner in range(pivot):
            diag_value = diag_value - upper[inner][pivot] * upper[inner][pivot]
        root_value = jnp.sqrt(diag_value)
        upper[pivot][pivot] = root_value
        for later in range(pivot + 1, order_size):
            entry = gram_matrix[pivot, later]
            for inner in range(pivot):
                entry = entry - upper[inner][pivot] * upper[inner][later]
            upper[pivot][later] = entry / root_value
    return jnp.stack([jnp.stack(row_list) for row_list in upper])

def upper_inverse(triangle):
    order_size = triangle.shape[0]
    zero_entry = jnp.zeros((), triangle.dtype)
    inverse = [[zero_entry for col_index in range(order_size)] for row_index in range(order_size)]
    for target in range(order_size):
        inverse[target][target] = 1.0 / triangle[target, target]
        for row_index in range(target - 1, -1, -1):
            entry = zero_entry
            for inner in range(row_index + 1, target + 1):
                entry = entry + triangle[row_index, inner] * inverse[inner][target]
            inverse[row_index][target] = -entry / triangle[row_index, row_index]
    return jnp.stack([jnp.stack(row_list) for row_list in inverse])

def combine_vectors(krylov, mixing):
    return jnp.einsum('kbj,kl->lbj', krylov, mixing, precision=highest)

def extended_fields(fields, send_rows):
    send_list = send_rows.reshape(N_DOM, N_COL, HALO)
    picked = jax.vmap(jax.vmap(lambda vector_in, row_list: vector_in[row_list]))(fields, send_list)
    zero_faces = jnp.zeros_like(picked[:, :1, :FACE])
    from_lower = jnp.concatenate([zero_faces, picked[:, :-1, FACE:2 * FACE]], axis=1)
    from_upper = jnp.concatenate([picked[:, 1:, :FACE], zero_faces], axis=1)
    pieces = [fields, from_lower, from_upper]
    for level_index in range(LEVELS):
        partners = jnp.bitwise_xor(jnp.arange(N_DOM, dtype=jnp.int32), 1 << level_index)
        first_block = (2 + level_index) * FACE
        pieces.append(picked[partners][:, :, first_block:first_block + FACE])
    return jnp.concatenate(pieces, axis=2)

def apply_operator(fields, diag_blocks, couplings, columns, send_rows):
    device_count = N_DOM * N_COL
    own_term = lax.map(lambda device_pair: jnp.einsum('rij,rj->ri', device_pair[0].astype(jnp.float32), device_pair[1], precision=highest), (diag_blocks.reshape(device_count, RB, BS, BS), fields.reshape(device_count, RB, BS)))
    extended = extended_fields(fields.reshape(N_DOM, N_COL, RB, BS), send_rows)
    neighbour_blocks = jax.vmap(jax.vmap(lambda ext_rows, col_list: ext_rows[col_list]))(extended, columns.reshape(N_DOM, N_COL, RB, NEIGH))
    neighbour_blocks = neighbour_blocks.reshape(BLOCKS, NEIGH, BS)
    return own_term.reshape(BLOCKS, BS) + lax.optimization_barrier(jnp.sum(couplings.astype(jnp.float32) * neighbour_blocks, axis=1))

def reference(diag_blocks, couplings, columns, send_rows, shifts, start_vector, sketch):
    device_count = N_DOM * N_COL
    vectors = [start_vector]
    for power_index in range(S):
        vectors.append(apply_operator(vectors[-1], diag_blocks, couplings, columns, send_rows) - shifts[power_index] * vectors[-1])
    krylov = jnp.stack(vectors)
    krylov_dev = jnp.moveaxis(krylov.reshape(VECS, device_count, RB, BS), 1, 0)
    sketch_dev = jnp.moveaxis(sketch.reshape(SKETCH, device_count, RB, BS), 1, 0)
    partials = lax.map(lambda device_pair: jnp.einsum('krj,srj->ks', device_pair[0], device_pair[1].astype(jnp.float32), precision=highest), (krylov_dev, sketch_dev))
    sketched = lax.optimization_barrier(jnp.sum(partials, axis=0))
    sketch_factor = cholesky_upper(jnp.dot(sketched, sketched.T, precision=highest))
    whitened = combine_vectors(krylov, upper_inverse(sketch_factor))
    gram_matrix = jnp.einsum('kbj,lbj->kl', whitened, whitened, precision=highest) / ROWS
    gram_factor = cholesky_upper(gram_matrix)
    orthonormal = combine_vectors(whitened, upper_inverse(gram_factor))
    factor = jnp.dot(gram_factor, sketch_factor, precision=highest)
    return (orthonormal, factor, sketch_factor)
```

```python
import functools

import jax
import jax.numpy as jnp
from jax import lax
from jax.experimental import pallas as pl
from jax.experimental.pallas import tpu as pltpu
from jax.sharding import PartitionSpec as P

f32, bf16, i32 = jnp.float32, jnp.bfloat16, jnp.int32
VMEM = pl.BlockSpec(memory_space=pltpu.VMEM)
SUB, LANE = 8, 128
HI_LANE, LO_LANE = 32, 64


def params():
    return pltpu.CompilerParams(vmem_limit_bytes=16 << 20)


def run(body, outs, args, name, cost=(0, 0), scratch=()):
    return pl.pallas_call(
        body,
        out_shape=[jax.ShapeDtypeStruct(shape, dtype) for shape, dtype in outs],
        in_specs=[VMEM] * len(args),
        out_specs=[VMEM] * len(outs),
        scratch_shapes=list(scratch),
        compiler_params=params(),
        cost_estimate=pl.CostEstimate(flops=cost[0], bytes_accessed=cost[1], transcendentals=0),
        name=name,
    )(*args)


def lanes(shape=(SUB, LANE)):
    return lax.broadcasted_iota(i32, shape, len(shape) - 1)


def subs(shape=(SUB, LANE)):
    return lax.broadcasted_iota(i32, shape, len(shape) - 2)


def two_parts(value):
    high = value.astype(bf16)
    return high, (value - high.astype(f32)).astype(bf16)


def three_parts(value):
    high = value.astype(bf16)
    rest = value - high.astype(f32)
    middle = rest.astype(bf16)
    return high, middle, (rest - middle.astype(f32)).astype(bf16)


def dot(left, right):
    return lax.dot_general(left, right, (((1,), (0,)), ((), ())), preferred_element_type=f32)


def dot_nt(left, right):
    return lax.dot_general(left, right, (((1,), (1,)), ((), ())), preferred_element_type=f32)


def two_sum(a, b):
    total = a + b
    part = total - a
    return total, (a - (total - part)) + (b - part)


def split(a):
    scaled = a * 4097.0
    high = scaled - (scaled - a)
    return high, a - high


def two_product(a, a_split, b, b_split):
    product = a * b
    (ah, al), (bh, bl) = a_split, b_split
    return product, ((ah * bh - product) + ah * bl + al * bh) + al * bl


def pair_add(a, b):
    total, error = two_sum(a[0], b[0])
    return total, error + (a[1] + b[1])


def take_rows(send_hot, value):
    high, middle, low = three_parts(value)
    return dot(send_hot, high) + dot(send_hot, middle) + dot(send_hot, low)


def write_pieces(picked, out_refs):
    start = 0
    for ref in out_refs:
        ref[...] = picked[start : start + ref.shape[0]]
        start += ref.shape[0]


def first_body(send_ref, start_ref, hot_ref, *rest):
    out_refs, row_ref = rest[:-1], rest[-1]
    sends = send_ref.shape[1]
    row_ref[...] = jnp.full((SUB, LANE), -1, i32)
    row_ref[0:1, 0:sends] = send_ref[...]
    wanted = jnp.broadcast_to(row_ref[0:1, :], (LANE, LANE))
    hot = jnp.where(wanted == subs((LANE, LANE)), 1.0, 0.0).astype(f32).T
    hot = hot[: hot_ref.shape[0], : hot_ref.shape[1]].astype(bf16)
    hot_ref[...] = hot
    write_pieces(take_rows(hot, start_ref[...]), out_refs)


def prepare_body(own_rows, face, swap, columns_ref, couplings_ref, shifts_ref, place_ref, hot_ref, wide_ref, shift_ref):
    neighbours = columns_ref.shape[1]
    columns = columns_ref[...]
    if swap:
        place = place_ref[0]
        lower = (columns >= own_rows) & (columns < own_rows + face)
        upper = (columns >= own_rows + face) & (columns < own_rows + 2 * face)
        columns = jnp.where(
            lower,
            jnp.where(place == 1, columns + face, -1),
            jnp.where(upper, jnp.where(place == 0, columns - face, -1), columns),
        )
    width = lanes((own_rows, LANE))
    couplings = couplings_ref[...].astype(f32)
    for k in range(neighbours):
        hot = jnp.where(columns[:, k : k + 1] == width, 1.0, 0.0).astype(bf16)
        hot_ref[k * own_rows : (k + 1) * own_rows, 0:LANE] = hot
        hot_ref[k * own_rows : (k + 1) * own_rows, LANE : 2 * LANE] = hot
        wide_ref[k] = couplings[:, k, :]
    for k in range(shift_ref.shape[0]):
        shift_ref[k] = jnp.broadcast_to(shifts_ref[0:1, k : k + 1], (SUB, LANE))


def matvec(blocks_ref, vector_ref, own_ref):
    groups = vector_ref.shape[0] // SUB

    def group(g, carry):
        base = pl.multiple_of(g * SUB, SUB)
        high, low = two_parts(vector_ref[pl.ds(base, SUB), :])
        left = jnp.concatenate([high.astype(f32), low.astype(f32)], axis=0).astype(bf16)
        sub = subs()
        total = jnp.zeros((SUB, LANE), f32)
        for b in range(0, SUB, 2):
            start = pl.multiple_of((g * SUB + b) * LANE, 2 * LANE)
            out = dot_nt(left, blocks_ref[pl.ds(start, 2 * LANE), :])
            both = out[:SUB] + out[SUB:]
            total = jnp.where(sub == b, both[:, :LANE], total)
            total = jnp.where(sub == b + 1, both[:, LANE:], total)
        own_ref[pl.ds(base, SUB), :] = total
        return carry

    lax.fori_loop(0, groups, group, 0)


def statistics(k, vectors, sketch_ref, packet_in, packet_ref, scratch_ref):
    rows = vectors[0].shape[0]
    groups = rows // SUB
    sketches = sketch_ref.shape[0]
    lane, sub = lanes(), subs()
    newest = [vectors[k][g * SUB : (g + 1) * SUB, :] for g in range(groups)]
    new_split = [split(x) for x in newest]

    def one(i, carry):
        row = sketch_ref[i].astype(f32)
        parts = [newest[g] * row[g * SUB : (g + 1) * SUB, :] for g in range(groups)]
        while len(parts) > 1:
            parts = [a + b for a, b in zip(parts[::2], parts[1::2])] + parts[len(parts) // 2 * 2 :]
        scratch_ref[pl.ds(pl.multiple_of(i * SUB, SUB), SUB), :] = parts[0]
        return carry

    lax.fori_loop(0, sketches, one, 0, unroll=4)
    partial = scratch_ref[...]
    ones = jnp.ones((SUB, LANE), bf16)
    high, middle, low = three_parts(partial)
    across = dot_nt(ones, high) + dot_nt(ones, middle) + dot_nt(ones, low)
    width = sketches * SUB
    pick = jnp.where(
        lax.broadcasted_iota(i32, (width, LANE), 0) // SUB == lax.broadcasted_iota(i32, (width, LANE), 1), 1.0, 0.0
    ).astype(bf16)
    high, middle, low = three_parts(across)
    sketch_row = dot(high, pick) + dot(middle, pick) + dot(low, pick)

    wide = (jnp.zeros((SUB, LANE), f32), jnp.zeros((SUB, LANE), f32))
    for l in range(k + 1):
        total = None
        for g in range(groups):
            other = vectors[l][g * SUB : (g + 1) * SUB, :] if l < k else newest[g]
            other_split = split(other) if l < k else new_split[g]
            product = two_product(newest[g], new_split[g], other, other_split)
            total = product if total is None else pair_add(total, product)
        for step in (4, 2, 1):
            total = pair_add(total, tuple(pltpu.roll(x, step, 0) for x in total))
        wide = tuple(jnp.where(sub == l, t, w) for t, w in zip(total, wide))
    for step in (64, 32, 16, 8, 4, 2, 1):
        wide = pair_add(wide, tuple(pltpu.roll(x, step, 1) for x in wide))
    wide = two_sum(*wide)

    packet = packet_in
    row_k = sub == k
    packet = jnp.where(row_k & (lane < sketches), sketch_row, packet)
    for part, first in zip(wide, (HI_LANE, LO_LANE)):
        column = lane == first + k
        packet = jnp.where(column & (sub <= k), part, packet)
        turned = jnp.where(lane == first + sub, part, 0.0)
        for step in (4, 2, 1):
            turned = turned + pltpu.roll(turned, step, 0)
        packet = jnp.where(row_k & (lane >= first) & (lane <= first + k), turned, packet)
    packet_ref[...] = packet


def middle_body(k, first, last, *refs):
    refs = list(refs)
    vectors = [refs.pop(0) for _ in range(k + 1)]
    sketch_ref = refs.pop(0)
    packet_in = jnp.zeros((SUB, LANE), f32) if first else refs.pop(0)[...]
    if not last:
        blocks_ref = refs.pop(0)
    packet_ref = refs.pop(0)
    own_ref = None if last else refs.pop(0)
    scratch_ref = refs.pop(0)
    if not last:
        matvec(blocks_ref, vectors[k], own_ref)
    statistics(k, vectors, sketch_ref, packet_in, packet_ref, scratch_ref)


def next_body(k, received, last, *refs):
    own_ref, vector_ref, hot_ref, wide_ref, shift_ref = refs[:5]
    refs = refs[5:]
    if not last:
        send_ref, refs = refs[0], refs[1:]
    halo_refs, refs = refs[:received], refs[received:]
    next_ref, refs = refs[0], refs[1:]
    out_refs, extended_ref = refs[:-1], refs[-1]
    rows = vector_ref.shape[0]
    extended_ref[0:rows, :] = vector_ref[...]
    start = rows
    for ref in halo_refs:
        extended_ref[start : start + ref.shape[0], :] = ref[...]
        start += ref.shape[0]
    if start < LANE:
        extended_ref[start:LANE, :] = jnp.zeros((LANE - start, LANE), f32)
    parts = jnp.concatenate(two_parts(extended_ref[...]), axis=0)
    gathered = dot(hot_ref[...], parts)
    shift = shift_ref[k]
    for g in range(rows // SUB):
        at = slice(g * SUB, (g + 1) * SUB)
        total = own_ref[at, :] - shift * vector_ref[at, :]
        for n in range(wide_ref.shape[0]):
            total = total + wide_ref[n, at, :] * gathered[n * rows + g * SUB : n * rows + (g + 1) * SUB]
        next_ref[at, :] = total
    if not last:
        write_pieces(take_rows(send_ref[...], next_ref[...]), out_refs)


def splat(value, row, column):
    return jnp.broadcast_to(value[row : row + 1, column : column + 1], (SUB, LANE))


def cholesky(entries, n):
    work = {(i, j): entries[i, j] for i in range(n) for j in range(i, n)}
    upper, reciprocal = {}, []
    for p in range(n):
        root = jnp.sqrt(work[p, p])
        inverse = 1.0 / root
        reciprocal.append(inverse)
        upper[p, p] = root
        for j in range(p + 1, n):
            upper[p, j] = work[p, j] * inverse
        for i in range(p + 1, n):
            for j in range(i, n):
                work[i, j] = work[i, j] - upper[p, i] * upper[p, j]
    return upper, reciprocal


def upper_inverse(upper, reciprocal, n):
    result = {}
    for j in range(n):
        result[j, j] = reciprocal[j]
        for i in range(j - 1, -1, -1):
            total = upper[i, j] * result[j, j]
            for m in range(i + 1, j):
                total = total + upper[i, m] * result[m, j]
            result[i, j] = -(total * reciprocal[i])
    return result


def upper_product(left, right, n):
    result = {}
    for i in range(n):
        for j in range(i, n):
            total = left[i, i] * right[i, j]
            for m in range(i + 1, j + 1):
                total = total + left[i, m] * right[m, j]
            result[i, j] = total
    return result


def laid_out(entries, n, by_row=True):
    lane, sub = lanes(), subs()
    rows = jnp.zeros((SUB, LANE), f32)
    for i in range(n):
        row = jnp.zeros((SUB, LANE), f32)
        for j in range(i, n):
            row = jnp.where(lane == j, entries[i, j], row)
        rows = jnp.where(sub == i, row, rows)
    return rows


def times_pair(pair, factor, factor_split):
    product, error = two_product(pair[0], split(pair[0]), factor, factor_split)
    return product, error + pair[1] * factor


def last_body(n, sketches, total_rows, packets_ref, *refs):
    vector_refs, (orthonormal_ref, factor_ref, sketch_factor_ref) = refs[:n], refs[n:]
    lane, sub = lanes(), subs()
    devices = packets_ref.shape[0] // SUB
    sums = [(packets_ref[i * SUB : (i + 1) * SUB, :], jnp.zeros((SUB, LANE), f32)) for i in range(devices)]
    while len(sums) > 1:
        sums = [pair_add(a, b) for a, b in zip(sums[::2], sums[1::2])] + sums[len(sums) // 2 * 2 :]
    total, error = sums[0]
    low_parts = pltpu.roll(total + error, LANE - (LO_LANE - HI_LANE), 1)
    gram = two_sum(total, error + low_parts)

    sketched = jnp.where(lane < sketches, total + error, 0.0)
    entries = {}
    for j in range(n):
        products = jnp.sum(sketched * jnp.broadcast_to(sketched[j : j + 1, :], (SUB, LANE)), axis=1, keepdims=True)
        column = jnp.broadcast_to(products, (SUB, LANE))
        for i in range(j + 1):
            entries[i, j] = jnp.broadcast_to(column[i : i + 1, :], (SUB, LANE))
    sketch_upper, sketch_reciprocal = cholesky(entries, n)
    mixing = upper_inverse(sketch_upper, sketch_reciprocal, n)

    half = None
    for k in range(n):
        row = jnp.zeros((SUB, LANE), f32)
        for j in range(k, n):
            row = jnp.where(lane == j, mixing[k, j], row)
        column = tuple(jnp.broadcast_to(x[:, HI_LANE + k : HI_LANE + k + 1], (SUB, LANE)) for x in gram)
        term = times_pair(column, row, split(row))
        half = term if half is None else pair_add(half, term)
    half = two_sum(*half)
    white = None
    for i in range(n):
        column = jnp.zeros((SUB, LANE), f32)
        for j in range(i, n):
            column = jnp.where(sub == j, mixing[i, j], column)
        row = tuple(jnp.broadcast_to(x[i : i + 1, :], (SUB, LANE)) for x in half)
        term = times_pair(row, column, split(column))
        white = term if white is None else pair_add(white, term)
    white = (white[0] + white[1]) / total_rows
    entries = {(i, j): splat(white, i, j) for i in range(n) for j in range(i, n)}
    gram_upper, gram_reciprocal = cholesky(entries, n)
    weights = upper_product(mixing, upper_inverse(gram_upper, gram_reciprocal, n), n)

    for g in range(vector_refs[0].shape[0] // SUB):
        at = slice(g * SUB, (g + 1) * SUB)
        basis = [ref[at, :] for ref in vector_refs]
        for j in range(n):
            value = basis[0] * weights[0, j]
            for i in range(1, j + 1):
                value = value + basis[i] * weights[i, j]
            orthonormal_ref[j, at, :] = value
    factor_ref[...] = laid_out(upper_product(gram_upper, sketch_upper, n), n)[:n, :n]
    sketch_factor_ref[...] = laid_out(sketch_upper, n)[:n, :n]


def shards(diag_blocks, couplings, columns, send_rows, shifts, start_vector, sketch):
    dom, col = lax.axis_size("dom"), lax.axis_size("col")
    levels = dom.bit_length() - 1
    rows, width = start_vector.shape
    neighbours = couplings.shape[1]
    sends = send_rows.shape[1]
    face = sends // (2 + levels)
    powers = shifts.shape[0]
    n = powers + 1
    sketches = sketch.shape[0]
    swap = col == 2
    blocks = diag_blocks.reshape(rows * width, width)
    pieces = [2 * face] if swap else [face, face]
    pieces = pieces + [face] * levels
    piece_outs = [((size, width), f32) for size in pieces]
    send_pad = -(-sends // 16) * 16

    def exchange(outgoing):
        outgoing = list(outgoing)
        if swap:
            side = [lax.ppermute(outgoing[0], "col", [(0, 1), (1, 0)])]
            outgoing = outgoing[1:]
        else:
            up = [(i, i + 1) for i in range(col - 1)]
            side = [
                lax.ppermute(outgoing[1], "col", up),
                lax.ppermute(outgoing[0], "col", [(j, i) for i, j in up]),
            ]
            outgoing = outgoing[2:]
        far = [
            lax.ppermute(piece, "dom", [(i, i ^ (1 << level)) for i in range(dom)])
            for level, piece in enumerate(outgoing)
        ]
        return side + far

    send_hot, *outgoing = run(
        first_body,
        [((send_pad, rows), bf16)] + piece_outs,
        (send_rows, start_vector),
        "first",
        scratch=[pltpu.VMEM((SUB, LANE), i32)],
    )
    place = jnp.full((1, neighbours), lax.axis_index("col"), i32).reshape(1, 1, neighbours)
    neighbour_hot, wide, shift = run(
        functools.partial(prepare_body, rows, face, swap),
        [
            ((neighbours * rows, 2 * LANE), bf16),
            ((neighbours, rows, width), f32),
            ((powers, SUB, LANE), f32),
        ],
        (columns, couplings, shifts.reshape(1, powers), place),
        "prepare",
        cost=(4_000_000, 1_000_000),
    )
    vectors = [start_vector]
    packet = None
    for k in range(n):
        last = k == powers
        received = None if last else exchange(outgoing)
        args = (*vectors, sketch, *(() if packet is None else (packet,)), *(() if last else (blocks,)))
        result = run(
            functools.partial(middle_body, k, packet is None, last),
            [((SUB, LANE), f32)] + ([] if last else [((rows, width), f32)]),
            args,
            f"middle_{k}",
            cost=(20_000_000, 4_000_000),
            scratch=[pltpu.VMEM((sketches * SUB, LANE), f32)],
        )
        packet = result[0]
        if last:
            break
        final = k + 1 == powers
        args = (result[1], vectors[-1], neighbour_hot, wide, shift, *(() if final else (send_hot,)), *received)
        vector, *outgoing = run(
            functools.partial(next_body, k, len(received), final),
            [((rows, width), f32)] + ([] if final else piece_outs),
            args,
            f"next_{k}",
            cost=(1_000_000, 1_000_000),
            scratch=[pltpu.VMEM((LANE, LANE), f32)],
        )
        vectors.append(vector)

    everyone = ("dom", "col")
    packets = lax.all_to_all(jnp.tile(packet, (dom * col, 1)), everyone, 0, 0, tiled=True)
    orthonormal, factor, sketch_factor = run(
        functools.partial(last_body, n, sketches, float(rows * width * dom * col)),
        [((n, rows, width), f32), ((n, n), f32), ((n, n), f32)],
        (packets, *vectors),
        "last",
        cost=(5_000_000, 1_000_000),
    )
    return orthonormal, factor, sketch_factor


def solution(mesh):
    both = ("dom", "col")
    in_specs = (
        P(both, None, None),
        P(both, None, None),
        P(both, None),
        P(both, None),
        P(),
        P(both, None),
        P(None, both, None),
    )
    out_specs = (P(None, both, None), P(), P())
    return jax.shard_map(shards, mesh=mesh, in_specs=in_specs, out_specs=out_specs, check_vma=False)
```

```python
import functools

import jax
import jax.numpy as jnp
from jax import lax
from jax.experimental import pallas as pl
from jax.experimental.pallas import tpu as pltpu
from jax.sharding import PartitionSpec as P

f32, bf16, i32 = jnp.float32, jnp.bfloat16, jnp.int32
VMEM = pl.BlockSpec(memory_space=pltpu.VMEM)
SUB, LANE = 8, 128
HI_LANE, LO_LANE = 32, 64


def params():
    return pltpu.CompilerParams(vmem_limit_bytes=16 << 20)


def run(body, outs, args, name, cost=(0, 0), scratch=()):
    return pl.pallas_call(
        body,
        out_shape=[jax.ShapeDtypeStruct(shape, dtype) for shape, dtype in outs],
        in_specs=[VMEM] * len(args),
        out_specs=[VMEM] * len(outs),
        scratch_shapes=list(scratch),
        compiler_params=params(),
        cost_estimate=pl.CostEstimate(flops=cost[0], bytes_accessed=cost[1], transcendentals=0),
        name=name,
    )(*args)


def lanes(shape=(SUB, LANE)):
    return lax.broadcasted_iota(i32, shape, len(shape) - 1)


def subs(shape=(SUB, LANE)):
    return lax.broadcasted_iota(i32, shape, len(shape) - 2)


def two_parts(value):
    high = value.astype(bf16)
    return high, (value - high.astype(f32)).astype(bf16)


def three_parts(value):
    high = value.astype(bf16)
    rest = value - high.astype(f32)
    middle = rest.astype(bf16)
    return high, middle, (rest - middle.astype(f32)).astype(bf16)


def dot(left, right):
    return lax.dot_general(left, right, (((1,), (0,)), ((), ())), preferred_element_type=f32)


def dot_nt(left, right):
    return lax.dot_general(left, right, (((1,), (1,)), ((), ())), preferred_element_type=f32)


def two_sum(a, b):
    total = a + b
    part = total - a
    return total, (a - (total - part)) + (b - part)


def split(a):
    scaled = a * 4097.0
    high = scaled - (scaled - a)
    return high, a - high


def two_product(a, a_split, b, b_split):
    product = a * b
    (ah, al), (bh, bl) = a_split, b_split
    return product, ((ah * bh - product) + ah * bl + al * bh) + al * bl


def pair_add(a, b):
    total, error = two_sum(a[0], b[0])
    return total, error + (a[1] + b[1])


def take_rows(send_hot, value):
    high, middle, low = three_parts(value)
    return dot(send_hot, high) + dot(send_hot, middle) + dot(send_hot, low)


def write_pieces(picked, out_refs):
    start = 0
    for ref in out_refs:
        ref[...] = picked[start : start + ref.shape[0]]
        start += ref.shape[0]


def one_hot(row, rows):
    wanted = jnp.broadcast_to(row, (LANE, LANE))
    return jnp.where(wanted == subs((LANE, LANE)), 1.0, 0.0).astype(f32).T[:rows]


def first_body(sends_ref, vector_ref, hot_ref, *rest):
    out_refs, row_ref = rest[:-1], rest[-1]
    row_ref[...] = jnp.full((SUB, LANE), -1, i32)
    row_ref[0:1, 0 : sends_ref.shape[1]] = sends_ref[...]
    hot = one_hot(row_ref[0:1, :], hot_ref.shape[0])[:, : hot_ref.shape[1]].astype(bf16)
    hot_ref[...] = hot
    write_pieces(take_rows(hot, vector_ref[...]), out_refs)


def prepare(face, swap, columns_ref, couplings_ref, shifts_ref, place_ref, row_ref, hot_ref, wide_ref, shift_ref):
    neighbours, own_rows = columns_ref.shape
    row_ref[...] = jnp.full((SUB, LANE), -1, i32)
    row_ref[0:neighbours, 0:own_rows] = columns_ref[...]
    columns = row_ref[...]
    if swap:
        place = jnp.broadcast_to(place_ref[...], (SUB, LANE))
        lower = (columns >= own_rows) & (columns < own_rows + face)
        upper = (columns >= own_rows + face) & (columns < own_rows + 2 * face)
        columns = jnp.where(
            lower,
            jnp.where(place == 1, columns + face, -1),
            jnp.where(upper, jnp.where(place == 0, columns - face, -1), columns),
        )
    for k in range(neighbours):
        hot = one_hot(columns[k : k + 1, :], own_rows).astype(bf16)
        hot_ref[k * own_rows : (k + 1) * own_rows, 0:LANE] = hot
        hot_ref[k * own_rows : (k + 1) * own_rows, LANE : 2 * LANE] = hot
        wide_ref[k] = couplings_ref[k].astype(f32)
    for k in range(shift_ref.shape[0]):
        shift_ref[k] = jnp.broadcast_to(shifts_ref[0:1, k : k + 1], (SUB, LANE))


def matvec(blocks_ref, vector_ref, own_ref):
    sub = subs()
    for g in range(vector_ref.shape[0] // SUB):
        high, low = two_parts(vector_ref[g * SUB : (g + 1) * SUB, :])
        left = jnp.concatenate([high.astype(f32), low.astype(f32)], axis=0).astype(bf16)
        total = None
        for b in range(0, SUB, 2):
            start = (g * SUB + b) * LANE
            out = dot_nt(left, blocks_ref[start : start + 2 * LANE, :])
            both = out[:SUB] + out[SUB:]
            total = both[:, :LANE] if total is None else jnp.where(sub == b, both[:, :LANE], total)
            total = jnp.where(sub == b + 1, both[:, LANE:], total)
        own_ref[g * SUB : (g + 1) * SUB, :] = total


def statistics(k, vectors, sketch_ref, packet):
    rows = vectors[0].shape[0]
    groups = rows // SUB
    sketches = sketch_ref.shape[0]
    lane, sub = lanes(), subs()
    newest = [vectors[k][g * SUB : (g + 1) * SUB, :] for g in range(groups)]
    new_split = [split(x) for x in newest]

    sums = []
    for i in range(sketches):
        row = sketch_ref[i].astype(f32)
        parts = [newest[g] * row[g * SUB : (g + 1) * SUB, :] for g in range(groups)]
        while len(parts) > 1:
            parts = [a + b for a, b in zip(parts[::2], parts[1::2])] + parts[len(parts) // 2 * 2 :]
        sums.append(parts[0])
    high, middle, low = three_parts(jnp.concatenate(sums, axis=0))
    ones = jnp.ones((LANE, LANE), bf16)
    across = dot(high, ones) + dot(middle, ones) + dot(low, ones)
    picked = [jnp.where(lane == i, across[i * SUB : (i + 1) * SUB, :], 0.0) for i in range(sketches)]
    while len(picked) > 1:
        picked = [a + b for a, b in zip(picked[::2], picked[1::2])] + picked[len(picked) // 2 * 2 :]
    sketch_row = picked[0]
    for step in (4, 2, 1):
        sketch_row = sketch_row + pltpu.roll(sketch_row, step, 0)

    wide = (jnp.zeros((SUB, LANE), f32), jnp.zeros((SUB, LANE), f32))
    for l in range(k + 1):
        total = None
        for g in range(groups):
            other = vectors[l][g * SUB : (g + 1) * SUB, :] if l < k else newest[g]
            other_split = split(other) if l < k else new_split[g]
            product = two_product(newest[g], new_split[g], other, other_split)
            total = product if total is None else pair_add(total, product)
        for step in (4, 2, 1):
            total = pair_add(total, tuple(pltpu.roll(x, step, 0) for x in total))
        wide = tuple(jnp.where(sub == l, t, w) for t, w in zip(total, wide))
    for step in (64, 32, 16, 8, 4, 2, 1):
        wide = pair_add(wide, tuple(pltpu.roll(x, step, 1) for x in wide))
    wide = two_sum(*wide)

    row_k = sub == k
    packet = jnp.where(row_k & (lane < sketches), sketch_row, packet)
    for part, first in zip(wide, (HI_LANE, LO_LANE)):
        column = lane == first + k
        packet = jnp.where(column & (sub <= k), part, packet)
        turned = jnp.where(lane == first + sub, part, 0.0)
        for step in (4, 2, 1):
            turned = turned + pltpu.roll(turned, step, 0)
        packet = jnp.where(row_k & (lane >= first) & (lane <= first + k), turned, packet)
    return packet


def setup_body(face, swap, *refs):
    columns_ref, couplings_ref, shifts_ref, place_ref, blocks_ref, vector_ref = refs[:6]
    own_ref, hot_ref, wide_ref, shift_ref, row_ref = refs[6:]
    prepare(face, swap, columns_ref, couplings_ref, shifts_ref, place_ref, row_ref, hot_ref, wide_ref, shift_ref)
    matvec(blocks_ref, vector_ref, own_ref)


def middle_body(k, last, *refs):
    vectors, refs = refs[: k + 1], list(refs[k + 1 :])
    sketch_ref = refs.pop(0)
    packet = jnp.zeros((SUB, LANE), f32) if k == 1 else refs.pop(0)[...]
    if last:
        (packet_ref,) = refs
    else:
        blocks_ref, packet_ref, own_ref = refs
        matvec(blocks_ref, vectors[k], own_ref)
    for newest in range(0 if k == 1 else k, k + 1):
        packet = statistics(newest, vectors, sketch_ref, packet)
    packet_ref[...] = packet


def next_body(k, starts, last, *refs):
    own_ref, vector_ref, hot_ref, wide_ref, shift_ref = refs[:5]
    refs = refs[5:]
    if not last:
        send_ref, refs = refs[0], refs[1:]
    halo_refs, refs = refs[: len(starts)], refs[len(starts) :]
    next_ref, refs = refs[0], refs[1:]
    out_refs, extended_ref = refs[:-1], refs[-1]
    rows = vector_ref.shape[0]
    extended_ref[0:rows, :] = vector_ref[...]
    end = rows
    for start, ref in zip(starts, halo_refs):
        extended_ref[start : start + ref.shape[0], :] = ref[...]
        end += ref.shape[0]
    if end < LANE:
        extended_ref[end:LANE, :] = jnp.zeros((LANE - end, LANE), f32)
    parts = jnp.concatenate(two_parts(extended_ref[...]), axis=0)
    gathered = dot(hot_ref[...], parts)
    shift = shift_ref[k]
    for g in range(rows // SUB):
        at = slice(g * SUB, (g + 1) * SUB)
        total = own_ref[at, :] - shift * vector_ref[at, :]
        for n in range(wide_ref.shape[0]):
            total = total + wide_ref[n, at, :] * gathered[n * rows + g * SUB : n * rows + (g + 1) * SUB]
        next_ref[at, :] = total
    if not last:
        write_pieces(take_rows(send_ref[...], next_ref[...]), out_refs)


def splat(value, row, column):
    return jnp.broadcast_to(value[row : row + 1, column : column + 1], (SUB, LANE))


def cholesky(entries, n):
    work = {(i, j): entries[i, j] for i in range(n) for j in range(i, n)}
    upper, reciprocal = {}, []
    for p in range(n):
        root = jnp.sqrt(work[p, p])
        inverse = 1.0 / root
        reciprocal.append(inverse)
        upper[p, p] = root
        for j in range(p + 1, n):
            upper[p, j] = work[p, j] * inverse
        for i in range(p + 1, n):
            for j in range(i, n):
                work[i, j] = work[i, j] - upper[p, i] * upper[p, j]
    return upper, reciprocal


def upper_inverse(upper, reciprocal, n):
    result = {}
    for j in range(n):
        result[j, j] = reciprocal[j]
        for i in range(j - 1, -1, -1):
            total = upper[i, j] * result[j, j]
            for m in range(i + 1, j):
                total = total + upper[i, m] * result[m, j]
            result[i, j] = -(total * reciprocal[i])
    return result


def upper_product(left, right, n):
    result = {}
    for i in range(n):
        for j in range(i, n):
            total = left[i, i] * right[i, j]
            for m in range(i + 1, j + 1):
                total = total + left[i, m] * right[m, j]
            result[i, j] = total
    return result


def laid_out(entries, n, by_row=True):
    lane, sub = lanes(), subs()
    rows = jnp.zeros((SUB, LANE), f32)
    for i in range(n):
        row = jnp.zeros((SUB, LANE), f32)
        for j in range(i, n):
            row = jnp.where(lane == j, entries[i, j], row)
        rows = jnp.where(sub == i, row, rows)
    return rows


def times_pair(pair, factor, factor_split):
    product, error = two_product(pair[0], split(pair[0]), factor, factor_split)
    return product, error + pair[1] * factor


def last_body(n, sketches, total_rows, packets_ref, *refs):
    vector_refs, (orthonormal_ref, factor_ref, sketch_factor_ref) = refs[:n], refs[n:]
    lane, sub = lanes(), subs()
    devices = packets_ref.shape[0] // SUB
    sums = [(packets_ref[i * SUB : (i + 1) * SUB, :], jnp.zeros((SUB, LANE), f32)) for i in range(devices)]
    while len(sums) > 1:
        sums = [pair_add(a, b) for a, b in zip(sums[::2], sums[1::2])] + sums[len(sums) // 2 * 2 :]
    total, error = sums[0]
    low_parts = pltpu.roll(total + error, LANE - (LO_LANE - HI_LANE), 1)
    gram = two_sum(total, error + low_parts)

    sketched = jnp.where(lane < sketches, total + error, 0.0)
    entries = {}
    for j in range(n):
        products = jnp.sum(sketched * jnp.broadcast_to(sketched[j : j + 1, :], (SUB, LANE)), axis=1, keepdims=True)
        column = jnp.broadcast_to(products, (SUB, LANE))
        for i in range(j + 1):
            entries[i, j] = jnp.broadcast_to(column[i : i + 1, :], (SUB, LANE))
    sketch_upper, sketch_reciprocal = cholesky(entries, n)
    mixing = upper_inverse(sketch_upper, sketch_reciprocal, n)

    half = None
    for k in range(n):
        row = jnp.zeros((SUB, LANE), f32)
        for j in range(k, n):
            row = jnp.where(lane == j, mixing[k, j], row)
        column = tuple(jnp.broadcast_to(x[:, HI_LANE + k : HI_LANE + k + 1], (SUB, LANE)) for x in gram)
        term = times_pair(column, row, split(row))
        half = term if half is None else pair_add(half, term)
    half = two_sum(*half)
    white = None
    for i in range(n):
        column = jnp.zeros((SUB, LANE), f32)
        for j in range(i, n):
            column = jnp.where(sub == j, mixing[i, j], column)
        row = tuple(jnp.broadcast_to(x[i : i + 1, :], (SUB, LANE)) for x in half)
        term = times_pair(row, column, split(column))
        white = term if white is None else pair_add(white, term)
    white = (white[0] + white[1]) / total_rows
    entries = {(i, j): splat(white, i, j) for i in range(n) for j in range(i, n)}
    gram_upper, gram_reciprocal = cholesky(entries, n)
    weights = upper_product(mixing, upper_inverse(gram_upper, gram_reciprocal, n), n)

    for g in range(vector_refs[0].shape[0] // SUB):
        at = slice(g * SUB, (g + 1) * SUB)
        basis = [ref[at, :] for ref in vector_refs]
        for j in range(n):
            value = basis[0] * weights[0, j]
            for i in range(1, j + 1):
                value = value + basis[i] * weights[i, j]
            orthonormal_ref[j, at, :] = value
    factor_ref[...] = laid_out(upper_product(gram_upper, sketch_upper, n), n)[:n, :n]
    sketch_factor_ref[...] = laid_out(sketch_upper, n)[:n, :n]


def shards(diag_blocks, couplings, columns, send_rows, shifts, start_vector, sketch):
    dom, col = lax.axis_size("dom"), lax.axis_size("col")
    levels = dom.bit_length() - 1
    rows, width = start_vector.shape
    neighbours = couplings.shape[1]
    sends = send_rows.shape[1]
    face = sends // (2 + levels)
    powers = shifts.shape[0]
    n = powers + 1
    sketches = sketch.shape[0]
    swap = col == 2
    blocks = diag_blocks.reshape(rows * width, width)
    pieces = [2 * face] if swap else [face, face]
    pieces = pieces + [face] * levels
    piece_outs = [((size, width), f32) for size in pieces]
    starts = [rows + (2 + level) * face for level in reversed(range(levels))] + ([rows] if swap else [rows, rows + face])
    send_pad = -(-sends // 16) * 16

    def exchange(outgoing):
        side, far = list(outgoing[:-levels]), list(outgoing[-levels:])
        for level in reversed(range(levels)):
            far[level] = lax.ppermute(far[level], "dom", [(i, i ^ (1 << level)) for i in range(dom)])
        if swap:
            side = [lax.ppermute(side[0], "col", [(0, 1), (1, 0)])]
        else:
            up = [(i, i + 1) for i in range(col - 1)]
            down = [(j, i) for i, j in up]
            side = [lax.ppermute(side[1], "col", up), lax.ppermute(side[0], "col", down)]
        return far[::-1] + side

    send_hot, *outgoing = run(
        first_body,
        [((send_pad, rows), bf16)] + piece_outs,
        (send_rows, start_vector),
        "first",
        cost=(100_000_000_000, 1_000_000_000),
        scratch=[pltpu.VMEM((SUB, LANE), i32)],
    )
    vectors = [start_vector]
    place = jnp.full((1, LANE), lax.axis_index("col"), i32)
    received = exchange(outgoing)
    own, neighbour_hot, wide, shift = run(
        functools.partial(setup_body, face, swap),
        [
            ((rows, width), f32),
            ((neighbours * rows, 2 * LANE), bf16),
            ((neighbours, rows, width), f32),
            ((powers, SUB, LANE), f32),
        ],
        (columns.T, couplings.transpose(1, 0, 2), shifts.reshape(1, powers), place, blocks, start_vector),
        "setup",
        cost=(20_000_000, 4_000_000),
        scratch=[pltpu.VMEM((SUB, LANE), i32)],
    )
    packet = ()
    for k in range(powers):
        if k:
            received = exchange(outgoing)
            *packet, own = run(
                functools.partial(middle_body, k, False),
                [((SUB, LANE), f32), ((rows, width), f32)],
                (*vectors, sketch, *packet, blocks),
                f"middle_{k}",
                cost=(20_000_000, 4_000_000),
            )
        final = k + 1 == powers
        vector, *outgoing = run(
            functools.partial(next_body, k, starts, final),
            [((rows, width), f32)] + ([] if final else piece_outs),
            (own, vectors[-1], neighbour_hot, wide, shift, *(() if final else (send_hot,)), *received),
            f"next_{k}",
            cost=(1_000_000, 1_000_000),
            scratch=[pltpu.VMEM((LANE, LANE), f32)],
        )
        vectors.append(vector)
    (packet,) = run(
        functools.partial(middle_body, powers, True), [((SUB, LANE), f32)], (*vectors, sketch, *packet), "middle_last"
    )

    everyone = ("dom", "col")
    packets = lax.all_to_all(jnp.tile(packet, (dom * col, 1)), everyone, 0, 0, tiled=True)
    orthonormal, factor, sketch_factor = run(
        functools.partial(last_body, n, sketches, float(rows * width * dom * col)),
        [((n, rows, width), f32), ((n, n), f32), ((n, n), f32)],
        (packets, *vectors),
        "last",
        cost=(5_000_000, 1_000_000),
    )
    return orthonormal, factor, sketch_factor


def solution(mesh):
    both = ("dom", "col")
    in_specs = (
        P(both, None, None),
        P(both, None, None),
        P(both, None),
        P(both, None),
        P(),
        P(both, None),
        P(None, both, None),
    )
    out_specs = (P(None, both, None), P(), P())
    return jax.shard_map(shards, mesh=mesh, in_specs=in_specs, out_specs=out_specs, check_vma=False)
```

```python
import functools

import jax
import jax.numpy as jnp
from jax import lax
from jax.experimental import pallas as pl
from jax.experimental.pallas import tpu as pltpu
from jax.sharding import PartitionSpec as P


f32, bf16, i32 = jnp.float32, jnp.bfloat16, jnp.int32
VMEM = pl.BlockSpec(memory_space=pltpu.VMEM)
SUB, LANE = 8, 128
HI_LANE, LO_LANE = 32, 64


def params():
    return pltpu.CompilerParams(vmem_limit_bytes=16 << 20)


def run(body, outs, args, cost=(0, 0), scratch=()):
    return pl.pallas_call(
        body,
        out_shape=[jax.ShapeDtypeStruct(shape, dtype) for shape, dtype in outs],
        in_specs=[VMEM] * len(args),
        out_specs=[VMEM] * len(outs),
        scratch_shapes=list(scratch),
        compiler_params=params(),
        cost_estimate=pl.CostEstimate(flops=cost[0], bytes_accessed=cost[1], transcendentals=0),
    )(*args)


def lanes(shape=(SUB, LANE)):
    return lax.broadcasted_iota(i32, shape, len(shape) - 1)


def subs(shape=(SUB, LANE)):
    return lax.broadcasted_iota(i32, shape, len(shape) - 2)


def two_parts(value):
    high = value.astype(bf16)
    return high, (value - high.astype(f32)).astype(bf16)


def three_parts(value):
    high = value.astype(bf16)
    rest = value - high.astype(f32)
    middle = rest.astype(bf16)
    return high, middle, (rest - middle.astype(f32)).astype(bf16)


def dot(left, right):
    return lax.dot_general(left, right, (((1,), (0,)), ((), ())), preferred_element_type=f32)


def dot_nt(left, right):
    return lax.dot_general(left, right, (((1,), (1,)), ((), ())), preferred_element_type=f32)


def two_sum(a, b):
    total = a + b
    part = total - a
    return total, (a - (total - part)) + (b - part)


def split(a):
    scaled = a * 4097.0
    high = scaled - (scaled - a)
    return high, a - high


def two_product(a, a_split, b, b_split):
    product = a * b
    (ah, al), (bh, bl) = a_split, b_split
    return product, ((ah * bh - product) + ah * bl + al * bh) + al * bl


def pair_add(a, b):
    total, error = two_sum(a[0], b[0])
    return total, error + (a[1] + b[1])


def take_rows(send_hot, value):
    high, middle, low = three_parts(value)
    return dot(send_hot, high) + dot(send_hot, middle) + dot(send_hot, low)


def write_pieces(picked, out_refs):
    start = 0
    for ref in out_refs:
        ref[...] = picked[start : start + ref.shape[0]]
        start += ref.shape[0]


def one_hot(row, rows):
    wanted = jnp.broadcast_to(row, (LANE, LANE))
    return jnp.where(wanted == subs((LANE, LANE)), 1.0, 0.0).astype(f32).T[:rows]


def first_body(face, order, place_ref, sends_ref, vector_ref, hot_ref, *rest):
    out_refs, row_ref = rest[:-1], rest[-1]
    row_ref[...] = jnp.full((SUB, LANE), -1, i32)
    even = place_ref[0:1, 0:face] == 0
    for to, (source, odd_source) in enumerate(order):
        taken = sends_ref[:, source * face : (source + 1) * face]
        if odd_source != source:
            taken = jnp.where(even, taken, sends_ref[:, odd_source * face : (odd_source + 1) * face])
        row_ref[0:1, to * face : (to + 1) * face] = taken
    hot = one_hot(row_ref[0:1, :], hot_ref.shape[0])[:, : hot_ref.shape[1]].astype(bf16)
    hot_ref[...] = hot
    write_pieces(take_rows(hot, vector_ref[...]), out_refs)


def prepare(face, moves, columns_ref, couplings_ref, shifts_ref, place_ref, row_ref, hot_ref, wide_ref, shift_ref):
    neighbours, own_rows = columns_ref.shape
    row_ref[...] = jnp.full((SUB, LANE), -1, i32)
    row_ref[0:neighbours, 0:own_rows] = columns_ref[...]
    columns = row_ref[...]
    even = jnp.broadcast_to(place_ref[...], (SUB, LANE)) == 0
    moved = columns
    for source, targets in enumerate(moves):
        if targets == (source, source):
            continue
        first = own_rows + source * face
        to = [-1 if target is None else columns + (target - source) * face for target in targets]
        inside = (columns >= first) & (columns < first + face)
        moved = jnp.where(inside, jnp.where(even, to[0], to[1]), moved)
    columns = moved
    for k in range(neighbours):
        hot = one_hot(columns[k : k + 1, :], own_rows).astype(bf16)
        hot_ref[k * own_rows : (k + 1) * own_rows, 0:LANE] = hot
        hot_ref[k * own_rows : (k + 1) * own_rows, LANE : 2 * LANE] = hot
        wide_ref[k] = couplings_ref[k].astype(f32)
    for k in range(shift_ref.shape[0]):
        shift_ref[k] = jnp.broadcast_to(shifts_ref[0:1, k : k + 1], (SUB, LANE))


def matvec(blocks_ref, vector_ref, own_ref):
    sub = subs()
    for g in range(vector_ref.shape[0] // SUB):
        high, low = two_parts(vector_ref[g * SUB : (g + 1) * SUB, :])
        left = jnp.concatenate([high.astype(f32), low.astype(f32)], axis=0).astype(bf16)
        total = None
        for b in range(0, SUB, 2):
            start = (g * SUB + b) * LANE
            out = dot_nt(left, blocks_ref[start : start + 2 * LANE, :])
            both = out[:SUB] + out[SUB:]
            total = both[:, :LANE] if total is None else jnp.where(sub == b, both[:, :LANE], total)
            total = jnp.where(sub == b + 1, both[:, LANE:], total)
        own_ref[g * SUB : (g + 1) * SUB, :] = total


def statistics(k, vectors, sketch_ref, packet):
    rows = vectors[0].shape[0]
    groups = rows // SUB
    sketches = sketch_ref.shape[0]
    lane, sub = lanes(), subs()
    newest = [vectors[k][g * SUB : (g + 1) * SUB, :] for g in range(groups)]
    new_split = [split(x) for x in newest]

    sums = []
    for i in range(sketches):
        row = sketch_ref[i].astype(f32)
        parts = [newest[g] * row[g * SUB : (g + 1) * SUB, :] for g in range(groups)]
        while len(parts) > 1:
            parts = [a + b for a, b in zip(parts[::2], parts[1::2])] + parts[len(parts) // 2 * 2 :]
        sums.append(parts[0])
    high, middle, low = three_parts(jnp.concatenate(sums, axis=0))
    ones = jnp.ones((LANE, LANE), bf16)
    across = dot(high, ones) + dot(middle, ones) + dot(low, ones)
    picked = [jnp.where(lane == i, across[i * SUB : (i + 1) * SUB, :], 0.0) for i in range(sketches)]
    while len(picked) > 1:
        picked = [a + b for a, b in zip(picked[::2], picked[1::2])] + picked[len(picked) // 2 * 2 :]
    sketch_row = picked[0]
    for step in (4, 2, 1):
        sketch_row = sketch_row + pltpu.roll(sketch_row, step, 0)

    wide = (jnp.zeros((SUB, LANE), f32), jnp.zeros((SUB, LANE), f32))
    for l in range(k + 1):
        total = None
        for g in range(groups):
            other = vectors[l][g * SUB : (g + 1) * SUB, :] if l < k else newest[g]
            other_split = split(other) if l < k else new_split[g]
            product = two_product(newest[g], new_split[g], other, other_split)
            total = product if total is None else pair_add(total, product)
        for step in (4, 2, 1):
            total = pair_add(total, tuple(pltpu.roll(x, step, 0) for x in total))
        wide = tuple(jnp.where(sub == l, t, w) for t, w in zip(total, wide))
    for step in (64, 32, 16, 8, 4, 2, 1):
        wide = pair_add(wide, tuple(pltpu.roll(x, step, 1) for x in wide))
    wide = two_sum(*wide)

    row_k = sub == k
    packet = jnp.where(row_k & (lane < sketches), sketch_row, packet)
    for part, first in zip(wide, (HI_LANE, LO_LANE)):
        column = lane == first + k
        packet = jnp.where(column & (sub <= k), part, packet)
        turned = jnp.where(lane == first + sub, part, 0.0)
        for step in (4, 2, 1):
            turned = turned + pltpu.roll(turned, step, 0)
        packet = jnp.where(row_k & (lane >= first) & (lane <= first + k), turned, packet)
    return packet


def setup_body(face, moves, *refs):
    columns_ref, couplings_ref, shifts_ref, place_ref, blocks_ref, vector_ref = refs[:6]
    own_ref, hot_ref, wide_ref, shift_ref, row_ref = refs[6:]
    prepare(face, moves, columns_ref, couplings_ref, shifts_ref, place_ref, row_ref, hot_ref, wide_ref, shift_ref)
    matvec(blocks_ref, vector_ref, own_ref)


def middle_body(k, last, *refs):
    vectors, refs = refs[: k + 1], list(refs[k + 1 :])
    sketch_ref = refs.pop(0)
    packet = jnp.zeros((SUB, LANE), f32) if k == 1 else refs.pop(0)[...]
    if last:
        (packet_ref,) = refs
    else:
        blocks_ref, packet_ref, own_ref = refs
        matvec(blocks_ref, vectors[k], own_ref)
    for newest in range(0 if k == 1 else k, k + 1):
        packet = statistics(newest, vectors, sketch_ref, packet)
    packet_ref[...] = packet


def next_body(k, places, last, *refs):
    own_ref, vector_ref, hot_ref, wide_ref, shift_ref = refs[:5]
    refs = refs[5:]
    if not last:
        send_ref, refs = refs[0], refs[1:]
    halo_refs, refs = refs[: len(places)], refs[len(places) :]
    next_ref, refs = refs[0], refs[1:]
    out_refs, extended_ref = refs[:-1], refs[-1]
    rows = vector_ref.shape[0]
    extended_ref[0:rows, :] = vector_ref[...]
    for (first, count, to), ref in zip(places, halo_refs):
        extended_ref[to : to + count, :] = ref[first : first + count, :]
    end = rows + sum(count for _, count, _ in places)
    if end < LANE:
        extended_ref[end:LANE, :] = jnp.zeros((LANE - end, LANE), f32)
    parts = jnp.concatenate(two_parts(extended_ref[...]), axis=0)
    gathered = dot(hot_ref[...], parts)
    shift = shift_ref[k]
    for g in range(rows // SUB):
        at = slice(g * SUB, (g + 1) * SUB)
        total = own_ref[at, :] - shift * vector_ref[at, :]
        for n in range(wide_ref.shape[0]):
            total = total + wide_ref[n, at, :] * gathered[n * rows + g * SUB : n * rows + (g + 1) * SUB]
        next_ref[at, :] = total
    if not last:
        write_pieces(take_rows(send_ref[...], next_ref[...]), out_refs)


def splat(value, row, column):
    return jnp.broadcast_to(value[row : row + 1, column : column + 1], (SUB, LANE))


def cholesky(entries, n):
    work = {(i, j): entries[i, j] for i in range(n) for j in range(i, n)}
    upper, reciprocal = {}, []
    for p in range(n):
        root = jnp.sqrt(work[p, p])
        inverse = 1.0 / root
        reciprocal.append(inverse)
        upper[p, p] = root
        for j in range(p + 1, n):
            upper[p, j] = work[p, j] * inverse
        for i in range(p + 1, n):
            for j in range(i, n):
                work[i, j] = work[i, j] - upper[p, i] * upper[p, j]
    return upper, reciprocal


def upper_inverse(upper, reciprocal, n):
    result = {}
    for j in range(n):
        result[j, j] = reciprocal[j]
        for i in range(j - 1, -1, -1):
            total = upper[i, j] * result[j, j]
            for m in range(i + 1, j):
                total = total + upper[i, m] * result[m, j]
            result[i, j] = -(total * reciprocal[i])
    return result


def upper_product(left, right, n):
    result = {}
    for i in range(n):
        for j in range(i, n):
            total = left[i, i] * right[i, j]
            for m in range(i + 1, j + 1):
                total = total + left[i, m] * right[m, j]
            result[i, j] = total
    return result


def laid_out(entries, n):
    lane, sub = lanes(), subs()
    rows = jnp.zeros((SUB, LANE), f32)
    for i in range(n):
        row = jnp.zeros((SUB, LANE), f32)
        for j in range(i, n):
            row = jnp.where(lane == j, entries[i, j], row)
        rows = jnp.where(sub == i, row, rows)
    return rows


def times_pair(pair, factor, factor_split):
    product, error = two_product(pair[0], split(pair[0]), factor, factor_split)
    return product, error + pair[1] * factor


def last_body(n, sketches, total_rows, packets_ref, *refs):
    vector_refs, (orthonormal_ref, factor_ref, sketch_factor_ref) = refs[:n], refs[n:]
    lane, sub = lanes(), subs()
    devices = packets_ref.shape[0] // SUB
    sums = [(packets_ref[i * SUB : (i + 1) * SUB, :], jnp.zeros((SUB, LANE), f32)) for i in range(devices)]
    while len(sums) > 1:
        sums = [pair_add(a, b) for a, b in zip(sums[::2], sums[1::2])] + sums[len(sums) // 2 * 2 :]
    total, error = sums[0]
    low_parts = pltpu.roll(total + error, LANE - (LO_LANE - HI_LANE), 1)
    gram = two_sum(total, error + low_parts)

    sketched = jnp.where(lane < sketches, total + error, 0.0)
    entries = {}
    for j in range(n):
        products = jnp.sum(sketched * jnp.broadcast_to(sketched[j : j + 1, :], (SUB, LANE)), axis=1, keepdims=True)
        column = jnp.broadcast_to(products, (SUB, LANE))
        for i in range(j + 1):
            entries[i, j] = jnp.broadcast_to(column[i : i + 1, :], (SUB, LANE))
    sketch_upper, sketch_reciprocal = cholesky(entries, n)
    mixing = upper_inverse(sketch_upper, sketch_reciprocal, n)

    half = None
    for k in range(n):
        row = jnp.zeros((SUB, LANE), f32)
        for j in range(k, n):
            row = jnp.where(lane == j, mixing[k, j], row)
        column = tuple(jnp.broadcast_to(x[:, HI_LANE + k : HI_LANE + k + 1], (SUB, LANE)) for x in gram)
        term = times_pair(column, row, split(row))
        half = term if half is None else pair_add(half, term)
    half = two_sum(*half)
    white = None
    for i in range(n):
        column = jnp.zeros((SUB, LANE), f32)
        for j in range(i, n):
            column = jnp.where(sub == j, mixing[i, j], column)
        row = tuple(jnp.broadcast_to(x[i : i + 1, :], (SUB, LANE)) for x in half)
        term = times_pair(row, column, split(column))
        white = term if white is None else pair_add(white, term)
    white = (white[0] + white[1]) / total_rows
    entries = {(i, j): splat(white, i, j) for i in range(n) for j in range(i, n)}
    gram_upper, gram_reciprocal = cholesky(entries, n)
    weights = upper_product(mixing, upper_inverse(gram_upper, gram_reciprocal, n), n)

    for g in range(vector_refs[0].shape[0] // SUB):
        at = slice(g * SUB, (g + 1) * SUB)
        basis = [ref[at, :] for ref in vector_refs]
        for j in range(n):
            value = basis[0] * weights[0, j]
            for i in range(1, j + 1):
                value = value + basis[i] * weights[i, j]
            orthonormal_ref[j, at, :] = value
    factor_ref[...] = laid_out(upper_product(gram_upper, sketch_upper, n), n)[:n, :n]
    sketch_factor_ref[...] = laid_out(sketch_upper, n)[:n, :n]


def with_relay(col, levels):
    return col == 2 and levels >= 2


def shards(diag_blocks, couplings, columns, send_rows, shifts, start_vector, sketch):
    dom, col = lax.axis_size("dom"), lax.axis_size("col")
    levels = dom.bit_length() - 1
    rows, width = start_vector.shape
    neighbours = couplings.shape[1]
    sends = send_rows.shape[1]
    face = sends // (2 + levels)
    powers = shifts.shape[0]
    n = powers + 1
    sketches = sketch.shape[0]
    blocks = diag_blocks.reshape(rows * width, width)
    relay = with_relay(col, levels)

    near, far = 2 + levels - 2, 2 + levels - 1
    direct = list(range(2, near)) if relay else list(range(2, 2 + levels))
    if relay:
        sizes = [3, 2] + [1] * len(direct)
        order = [(0, 0), (1, 1), (far, near), (near, far), (near, far)] + [(x, x) for x in direct]
        count = 2 + len(direct)
        moves = [(None, 1), (0, None)] + [(x, x) for x in direct] + [(count, count + 1), (count + 1, count)]
        places = [(0, face, rows + x * face) for x in direct]
        places += [(0, 2 * face, rows), (0, face, rows + count * face), (face, face, rows + (count + 1) * face)]
    else:
        sizes = [1] * (2 + levels)
        order = [(x, x) for x in range(2 + levels)]
        moves = order
        places = [(0, face, rows + x * face) for x in direct[::-1] + [0, 1]]
    piece_outs = [((size * face, width), f32) for size in sizes]
    send_pad = -(-len(order) * face // 16) * 16

    def with_partner(piece, level):
        return lax.ppermute(piece, "dom", [(i, i ^ (1 << level)) for i in range(dom)])

    def exchange_relay(outgoing, k):
        side, pair, *rest = outgoing
        swapped = [(0, 1), (1, 0)]
        side = lax.ppermute(side, "col", swapped)
        received = []
        for x, piece in zip(direct, rest):
            received.append(with_partner(piece, x - 2))
        pair = lax.dynamic_update_slice(pair, side[2 * face :], (face, 0))
        far_pairs = [
            (i * 2 + c, (i ^ (1 << (near - 2 + c))) * 2 + c) for i in range(dom) for c in range(2)
        ]
        pair = lax.ppermute(pair, ("dom", "col"), far_pairs)
        relayed = lax.ppermute(pair, "col", swapped)
        return received + [side, pair, relayed]

    def exchange_direct(outgoing, k):
        up = [(i, i + 1) for i in range(col - 1)]
        received = [with_partner(outgoing[x], x - 2) for x in direct[::-1]]
        lower = lax.ppermute(outgoing[1], "col", up)
        return received + [lower, lax.ppermute(outgoing[0], "col", [(j, i) for i, j in up])]

    exchange = exchange_relay if relay else exchange_direct

    place = jnp.full((1, LANE), lax.axis_index("col"), i32)
    send_hot, *outgoing = run(
        functools.partial(first_body, face, order),
        [((send_pad, rows), bf16)] + piece_outs,
        (place, send_rows, start_vector),
        cost=(100_000_000_000, 1_000_000_000),
        scratch=[pltpu.VMEM((SUB, LANE), i32)],
    )
    vectors = [start_vector]
    packet = ()
    for k in range(powers):
        final = k + 1 == powers
        received = exchange(outgoing, k)
        if k == 0:
            own, neighbour_hot, wide, shift = run(
                functools.partial(setup_body, face, moves),
                [
                    ((rows, width), f32),
                    ((neighbours * rows, 2 * LANE), bf16),
                    ((neighbours, rows, width), f32),
                    ((powers, SUB, LANE), f32),
                ],
                (columns.T, couplings.transpose(1, 0, 2), shifts.reshape(1, powers), place, blocks, start_vector),
                cost=(20_000_000, 4_000_000),
                scratch=[pltpu.VMEM((SUB, LANE), i32)],
            )
        else:
            *packet, own = run(
                functools.partial(middle_body, k, False),
                [((SUB, LANE), f32), ((rows, width), f32)],
                (*vectors, sketch, *packet, blocks),
                cost=(20_000_000, 4_000_000),
            )
        vector, *outgoing = run(
            functools.partial(next_body, k, places, final),
            [((rows, width), f32)] + ([] if final else piece_outs),
            (own, vectors[-1], neighbour_hot, wide, shift, *(() if final else (send_hot,)), *received),
            cost=(1_000_000, 1_000_000),
            scratch=[pltpu.VMEM((LANE, LANE), f32)],
        )
        vectors.append(vector)
    (packet,) = run(functools.partial(middle_body, powers, True), [((SUB, LANE), f32)], (*vectors, sketch, *packet))

    everyone = ("dom", "col")
    packets = lax.all_to_all(jnp.tile(packet, (dom * col, 1)), everyone, 0, 0, tiled=True)
    orthonormal, factor, sketch_factor = run(
        functools.partial(last_body, n, sketches, float(rows * width * dom * col)),
        [((n, rows, width), f32), ((n, n), f32), ((n, n), f32)],
        (packets, *vectors),
        cost=(5_000_000, 1_000_000),
    )
    return orthonormal, factor, sketch_factor


def solution(mesh):
    both = ("dom", "col")
    in_specs = (
        P(both, None, None),
        P(both, None, None),
        P(both, None),
        P(both, None),
        P(),
        P(both, None),
        P(None, both, None),
    )
    out_specs = (P(None, both, None), P(), P())
    return jax.shard_map(shards, mesh=mesh, in_specs=in_specs, out_specs=out_specs, check_vma=False)
```

```python
import functools

import jax
import jax.numpy as jnp
from jax import lax
from jax.experimental import pallas as pl
from jax.experimental.pallas import tpu as pltpu
from jax.sharding import PartitionSpec as P


f32, bf16, i32 = jnp.float32, jnp.bfloat16, jnp.int32
VMEM = pl.BlockSpec(memory_space=pltpu.VMEM)
SUB, LANE = 8, 128
HI_LANE, LO_LANE = 64, 80
HALF, FOLD = 4, 32


def params():
    return pltpu.CompilerParams(vmem_limit_bytes=16 << 20)


def run(body, outs, args, cost=(0, 0), scratch=()):
    return pl.pallas_call(
        body,
        out_shape=[jax.ShapeDtypeStruct(shape, dtype) for shape, dtype in outs],
        in_specs=[VMEM] * len(args),
        out_specs=[VMEM] * len(outs),
        scratch_shapes=list(scratch),
        compiler_params=params(),
        cost_estimate=pl.CostEstimate(flops=cost[0], bytes_accessed=cost[1], transcendentals=0),
    )(*args)


def lanes(shape=(SUB, LANE)):
    return lax.broadcasted_iota(i32, shape, len(shape) - 1)


def subs(shape=(SUB, LANE)):
    return lax.broadcasted_iota(i32, shape, len(shape) - 2)


def two_parts(value):
    high = value.astype(bf16)
    return high, (value - high.astype(f32)).astype(bf16)


def three_parts(value):
    high = value.astype(bf16)
    rest = value - high.astype(f32)
    middle = rest.astype(bf16)
    return high, middle, (rest - middle.astype(f32)).astype(bf16)


def dot(left, right):
    return lax.dot_general(left, right, (((1,), (0,)), ((), ())), preferred_element_type=f32)


def dot_nt(left, right):
    return lax.dot_general(left, right, (((1,), (1,)), ((), ())), preferred_element_type=f32)


def two_sum(a, b):
    total = a + b
    part = total - a
    return total, (a - (total - part)) + (b - part)


def split(a):
    scaled = a * 4097.0
    high = scaled - (scaled - a)
    return high, a - high


def two_product(a, a_split, b_split):
    (ah, al), (bh, bl) = a_split, b_split
    return ah * bh, a * bl + al * bh


def pair_add(a, b):
    total, error = two_sum(a[0], b[0])
    return total, error + (a[1] + b[1])


def take_rows(send_hot, value):
    high, middle, low = three_parts(value)
    return dot(send_hot, high) + dot(send_hot, middle) + dot(send_hot, low)


def write_pieces(picked, out_refs):
    start = 0
    for ref in out_refs:
        ref[...] = picked[start : start + ref.shape[0]]
        start += ref.shape[0]


def one_hot(row, rows):
    wanted = jnp.broadcast_to(row, (LANE, LANE))
    return jnp.where(wanted == subs((LANE, LANE)), 1.0, 0.0).astype(f32).T[:rows]


def begin_body(place_ref, out_ref):
    out_ref[...] = place_ref[...]


def first_body(face, order, place_ref, sends_ref, vector_ref, hot_ref, sent_ref, *rest):
    out_refs, row_ref = rest[:-1], rest[-1]
    row_ref[...] = jnp.full((SUB, LANE), -1, i32)
    even = place_ref[0:1, 0:face] == 0
    for to, (source, odd_source) in enumerate(order):
        taken = sends_ref[:, source * face : (source + 1) * face]
        if odd_source != source:
            taken = jnp.where(even, taken, sends_ref[:, odd_source * face : (odd_source + 1) * face])
        row_ref[0:1, to * face : (to + 1) * face] = taken
    hot = one_hot(row_ref[0:1, :], hot_ref.shape[0])[:, : hot_ref.shape[1]].astype(bf16)
    hot_ref[...] = hot
    sent = take_rows(hot, vector_ref[...])
    sent_ref[...] = sent
    write_pieces(sent, out_refs)


def prepare(face, moves, columns_ref, couplings_ref, shifts_ref, place_ref, row_ref, hot_ref, wide_ref, shift_ref):
    neighbours, own_rows = columns_ref.shape
    row_ref[...] = jnp.full((SUB, LANE), -1, i32)
    row_ref[0:neighbours, 0:own_rows] = columns_ref[...]
    columns = row_ref[...]
    even = jnp.broadcast_to(place_ref[...], (SUB, LANE)) == 0
    moved = columns
    for source, targets in enumerate(moves):
        if targets == (source, source):
            continue
        first = own_rows + source * face
        to = [-1 if target is None else columns + (target - source) * face for target in targets]
        inside = (columns >= first) & (columns < first + face)
        moved = jnp.where(inside, jnp.where(even, to[0], to[1]), moved)
    columns = moved
    for k in range(neighbours):
        hot = one_hot(columns[k : k + 1, :], own_rows).astype(bf16)
        hot_ref[k * own_rows : (k + 1) * own_rows, 0:LANE] = hot
        hot_ref[k * own_rows : (k + 1) * own_rows, LANE : 2 * LANE] = hot
        wide_ref[k] = couplings_ref[k].astype(f32)
    for k in range(shift_ref.shape[0]):
        shift_ref[k] = jnp.broadcast_to(shifts_ref[0:1, k : k + 1], (SUB, LANE))


def matvec(blocks_ref, vector_ref, own_ref):
    sub = subs()
    for g in range(vector_ref.shape[0] // SUB):
        high, low = two_parts(vector_ref[g * SUB : (g + 1) * SUB, :])
        left = jnp.concatenate([high.astype(f32), low.astype(f32)], axis=0).astype(bf16)
        total = None
        for b in range(0, SUB, 2):
            start = (g * SUB + b) * LANE
            out = dot_nt(left, blocks_ref[start : start + 2 * LANE, :])
            both = out[:SUB] + out[SUB:]
            total = both[:, :LANE] if total is None else jnp.where(sub == b, both[:, :LANE], total)
            total = jnp.where(sub == b + 1, both[:, LANE:], total)
        own_ref[g * SUB : (g + 1) * SUB, :] = total


def statistics(k, vectors, sketch_ref, packet):
    rows = vectors[0].shape[0]
    groups = rows // SUB
    sketches = sketch_ref.shape[0]
    lane, sub = lanes(), subs()
    newest = [vectors[k][g * SUB : (g + 1) * SUB, :] for g in range(groups)]
    new_split = [split(x) for x in newest]

    sums = []
    for i in range(sketches):
        row = sketch_ref[i].astype(f32)
        parts = [newest[g] * row[g * SUB : (g + 1) * SUB, :] for g in range(groups)]
        while len(parts) > 1:
            parts = [a + b for a, b in zip(parts[::2], parts[1::2])] + parts[len(parts) // 2 * 2 :]
        sums.append(parts[0])
    high, middle, low = three_parts(jnp.concatenate(sums, axis=0))
    ones = jnp.ones((LANE, LANE), bf16)
    across = dot(high, ones) + dot(middle, ones) + dot(low, ones)
    picked = [jnp.where(lane == i, across[i * SUB : (i + 1) * SUB, :], 0.0) for i in range(sketches)]
    while len(picked) > 1:
        picked = [a + b for a, b in zip(picked[::2], picked[1::2])] + picked[len(picked) // 2 * 2 :]
    sketch_row = picked[0]
    for step in (4, 2, 1):
        sketch_row = sketch_row + pltpu.roll(sketch_row, step, 0)

    wide = (jnp.zeros((SUB, LANE), f32), jnp.zeros((SUB, LANE), f32))
    for l in range(k + 1):
        terms = []
        for g in range(groups):
            other_split = split(vectors[l][g * SUB : (g + 1) * SUB, :]) if l < k else new_split[g]
            terms.append(two_product(newest[g], new_split[g], other_split))
        while len(terms) > 1:
            terms = [pair_add(a, b) for a, b in zip(terms[::2], terms[1::2])] + terms[len(terms) // 2 * 2 :]
        total = terms[0]
        for step in (4, 2, 1):
            total = pair_add(total, tuple(pltpu.roll(x, step, 0) for x in total))
        wide = tuple(jnp.where(sub == l, t, w) for t, w in zip(total, wide))
    for step in (64, 32, 16, 8, 4, 2, 1):
        wide = pair_add(wide, tuple(pltpu.roll(x, step, 1) for x in wide))
    wide = two_sum(*wide)

    row_k = sub == k
    packet = jnp.where(row_k & (lane < sketches), sketch_row, packet)
    for part, first in zip(wide, (HI_LANE, LO_LANE)):
        packet = jnp.where((lane == first + k) & (sub <= k), part, packet)
        turned = jnp.where(lane == first + sub, part, 0.0)
        for step in (4, 2, 1):
            turned = turned + pltpu.roll(turned, step, 0)
        packet = jnp.where(row_k & (lane >= first) & (lane <= first + k), turned, packet)
    return packet


def setup_body(face, moves, *refs):
    columns_ref, couplings_ref, shifts_ref, place_ref, blocks_ref, vector_ref, send_ref, sent_ref = refs[:8]
    own_ref, base_ref, hot_ref, wide_ref, send_hot_ref, send_wide_ref, shift_ref, row_ref = refs[8:]
    prepare(face, moves, columns_ref, couplings_ref, shifts_ref, place_ref, row_ref, hot_ref, wide_ref, shift_ref)
    neighbours, rows = columns_ref.shape
    count = send_ref.shape[0]
    for k in range(neighbours):
        picked = dot(send_ref[...], hot_ref[k * rows : (k + 1) * rows, :])
        send_hot_ref[k * count : (k + 1) * count, :] = picked.astype(bf16)
        send_wide_ref[k] = dot(send_ref[...], couplings_ref[k])
    matvec(blocks_ref, vector_ref, own_ref)
    base_ref[...] = take_rows(send_ref[...], own_ref[...]) - shift_ref[0, 0:1, :] * sent_ref[...]


def matvec_body(k, blocks_ref, vector_ref, *refs):
    if len(refs) == 1:
        return matvec(blocks_ref, vector_ref, refs[0])
    send_ref, sent_ref, shift_ref, own_ref, base_ref = refs
    matvec(blocks_ref, vector_ref, own_ref)
    base_ref[...] = take_rows(send_ref[...], own_ref[...]) - shift_ref[k, 0:1, :] * sent_ref[...]


def sums_body(k, *refs):
    vectors, sketch_ref, refs = refs[: k + 1], refs[k + 1], refs[k + 2 :]
    packet = refs[0][...] if k else jnp.zeros((SUB, LANE), f32)
    refs[-1][...] = statistics(k, vectors, sketch_ref, packet)


def extend(places, vector_ref, halo_refs, extended_ref):
    rows = vector_ref.shape[0]
    extended_ref[0:rows, :] = vector_ref[...]
    for (first, count, to), ref in zip(places, halo_refs):
        extended_ref[to : to + count, :] = ref[first : first + count, :]
    end = rows + sum(count for _, count, _ in places)
    if end < LANE:
        extended_ref[end:LANE, :] = jnp.zeros((LANE - end, LANE), f32)
    return jnp.concatenate(two_parts(extended_ref[...]), axis=0)


def coupled(base, hot, wide_ref, parts):
    gathered = dot(hot, parts)
    count = base.shape[0]
    for n in range(wide_ref.shape[0]):
        base = base + wide_ref[n] * gathered[n * count : (n + 1) * count]
    return base


def sends_body(places, keep, *refs):
    base_ref, vector_ref, send_hot_ref, send_wide_ref = refs[:4]
    halo_refs, refs = refs[4 : 4 + len(places)], refs[4 + len(places) :]
    parts_ref, extended_ref, out_refs = refs[0], refs[-1], refs[1:-1]
    parts = extend(places, vector_ref, halo_refs, extended_ref)
    parts_ref[...] = parts
    sent = coupled(base_ref[...], send_hot_ref[...], send_wide_ref, parts)
    if keep:
        out_refs[0][...] = sent
        out_refs = out_refs[1:]
    write_pieces(sent, out_refs)


def rest_body(k, own_ref, vector_ref, hot_ref, wide_ref, shift_ref, parts_ref, next_ref):
    base = own_ref[...] - shift_ref[k, 0:1, :] * vector_ref[...]
    next_ref[...] = coupled(base, hot_ref[...], wide_ref, parts_ref[...])


def final_body(k, places, *refs):
    own_ref, hot_ref, wide_ref, shift_ref, sketch_ref, packet_ref = refs[:6]
    vectors, refs = refs[6 : 7 + k], refs[7 + k :]
    halo_refs, (next_ref, folded_ref, extended_ref) = refs[: len(places)], refs[len(places) :]
    vector_ref = vectors[-1]
    parts = extend(places, vector_ref, halo_refs, extended_ref)
    base = own_ref[...] - shift_ref[k, 0:1, :] * vector_ref[...]
    next_ref[...] = coupled(base, hot_ref[...], wide_ref, parts)
    packet = statistics(k + 1, [*vectors, next_ref], sketch_ref, packet_ref[...])
    folded_ref[...] = (packet + pltpu.roll(pltpu.roll(packet, HALF, 0), FOLD, 1))[:HALF]


def splat(value, row, column):
    return jnp.broadcast_to(value[row : row + 1, column : column + 1], (SUB, LANE))


def cholesky(entries, n):
    work = {(i, j): entries[i, j] for i in range(n) for j in range(i, n)}
    upper, reciprocal = {}, []
    for p in range(n):
        root = jnp.sqrt(work[p, p])
        inverse = 1.0 / root
        reciprocal.append(inverse)
        upper[p, p] = root
        for j in range(p + 1, n):
            upper[p, j] = work[p, j] * inverse
        for i in range(p + 1, n):
            for j in range(i, n):
                work[i, j] = work[i, j] - upper[p, i] * upper[p, j]
    return upper, reciprocal


def upper_inverse(upper, reciprocal, n):
    result = {}
    for j in range(n):
        result[j, j] = reciprocal[j]
        for i in range(j - 1, -1, -1):
            total = upper[i, j] * result[j, j]
            for m in range(i + 1, j):
                total = total + upper[i, m] * result[m, j]
            result[i, j] = -(total * reciprocal[i])
    return result


def upper_product(left, right, n):
    result = {}
    for i in range(n):
        for j in range(i, n):
            total = left[i, i] * right[i, j]
            for m in range(i + 1, j + 1):
                total = total + left[i, m] * right[m, j]
            result[i, j] = total
    return result


def laid_out(entries, n):
    lane, sub = lanes(), subs()
    rows = jnp.zeros((SUB, LANE), f32)
    for i in range(n):
        row = jnp.zeros((SUB, LANE), f32)
        for j in range(i, n):
            row = jnp.where(lane == j, entries[i, j], row)
        rows = jnp.where(sub == i, row, rows)
    return rows


def times_pair(pair, factor, factor_split):
    product, error = two_product(pair[0], split(pair[0]), factor_split)
    return product, error + pair[1] * factor


def last_body(n, sketches, total_rows, packets_ref, *refs):
    vector_refs, (orthonormal_ref, factor_ref, sketch_factor_ref) = refs[:n], refs[n:]
    lane, sub = lanes(), subs()
    sums = [(packets_ref[i : i + SUB, :], jnp.zeros((SUB, LANE), f32)) for i in range(0, packets_ref.shape[0], SUB)]
    while len(sums) > 1:
        sums = [pair_add(a, b) for a, b in zip(sums[::2], sums[1::2])] + sums[len(sums) // 2 * 2 :]
    folded = pair_add(sums[0], tuple(pltpu.roll(x, HALF, 0) for x in sums[0]))
    total, error = (jnp.where(sub < HALF, x, pltpu.roll(x, LANE - FOLD, 1)) for x in folded)
    low_parts = pltpu.roll(total + error, LANE - (LO_LANE - HI_LANE), 1)
    gram = two_sum(total, error + low_parts)

    sketched = jnp.where(lane < sketches, total + error, 0.0)
    entries = {}
    for j in range(n):
        products = jnp.sum(sketched * jnp.broadcast_to(sketched[j : j + 1, :], (SUB, LANE)), axis=1, keepdims=True)
        column = jnp.broadcast_to(products, (SUB, LANE))
        for i in range(j + 1):
            entries[i, j] = jnp.broadcast_to(column[i : i + 1, :], (SUB, LANE))
    sketch_upper, sketch_reciprocal = cholesky(entries, n)
    mixing = upper_inverse(sketch_upper, sketch_reciprocal, n)

    half = None
    for k in range(n):
        row = jnp.zeros((SUB, LANE), f32)
        for j in range(k, n):
            row = jnp.where(lane == j, mixing[k, j], row)
        at = HI_LANE + k
        column = tuple(jnp.broadcast_to(x[:, at : at + 1], (SUB, LANE)) for x in gram)
        term = times_pair(column, row, split(row))
        half = term if half is None else pair_add(half, term)
    half = two_sum(*half)
    white = None
    for i in range(n):
        column = jnp.zeros((SUB, LANE), f32)
        for j in range(i, n):
            column = jnp.where(sub == j, mixing[i, j], column)
        row = tuple(jnp.broadcast_to(x[i : i + 1, :], (SUB, LANE)) for x in half)
        term = times_pair(row, column, split(column))
        white = term if white is None else pair_add(white, term)
    white = (white[0] + white[1]) / total_rows
    entries = {(i, j): splat(white, i, j) for i in range(n) for j in range(i, n)}
    gram_upper, gram_reciprocal = cholesky(entries, n)
    weights = upper_product(mixing, upper_inverse(gram_upper, gram_reciprocal, n), n)

    for g in range(vector_refs[0].shape[0] // SUB):
        at = slice(g * SUB, (g + 1) * SUB)
        basis = [ref[at, :] for ref in vector_refs]
        for j in range(n):
            value = basis[0] * weights[0, j]
            for i in range(1, j + 1):
                value = value + basis[i] * weights[i, j]
            orthonormal_ref[j, at, :] = value
    factor_ref[...] = laid_out(upper_product(gram_upper, sketch_upper, n), n)[:n, :n]
    sketch_factor_ref[...] = laid_out(sketch_upper, n)[:n, :n]


def with_relay(col, levels):
    return col == 2 and levels >= 2


def shards(diag_blocks, couplings, columns, send_rows, shifts, start_vector, sketch):
    dom, col = lax.axis_size("dom"), lax.axis_size("col")
    levels = dom.bit_length() - 1
    rows, width = start_vector.shape
    neighbours = couplings.shape[1]
    sends = send_rows.shape[1]
    face = sends // (2 + levels)
    powers = shifts.shape[0]
    n = powers + 1
    sketches = sketch.shape[0]
    blocks = diag_blocks.reshape(rows * width, width)
    relay = with_relay(col, levels)

    near, far = 2 + levels - 2, 2 + levels - 1
    direct = list(range(2, near)) if relay else list(range(2, 2 + levels))
    if relay:
        sizes = [3, 2] + [1] * len(direct)
        order = [(0, 0), (1, 1), (far, near), (near, far), (near, far)] + [(x, x) for x in direct]
        count = 2 + len(direct)
        moves = [(None, 1), (0, None)] + [(x, x) for x in direct] + [(count, count + 1), (count + 1, count)]
        places = [(0, face, rows + x * face) for x in direct]
        places += [(0, 2 * face, rows), (0, face, rows + count * face), (face, face, rows + (count + 1) * face)]
    else:
        sizes = [1] * (2 + levels)
        order = [(x, x) for x in range(2 + levels)]
        moves = order
        places = [(0, face, rows + x * face) for x in direct[::-1] + [0, 1]]
    piece_outs = [((size * face, width), f32) for size in sizes]
    send_pad = -(-len(order) * face // 16) * 16

    def with_partner(piece, level):
        return lax.ppermute(piece, "dom", [(i, i ^ (1 << level)) for i in range(dom)])

    def exchange_relay(outgoing, k):
        side, pair, *rest = outgoing
        swapped = [(0, 1), (1, 0)]
        side = lax.ppermute(side, "col", swapped)
        received = []
        for x, piece in zip(direct, rest):
            received.append(with_partner(piece, x - 2))
        pair = lax.dynamic_update_slice(pair, side[2 * face :], (face, 0))
        far_pairs = [
            (i * 2 + c, (i ^ (1 << (near - 2 + c))) * 2 + c) for i in range(dom) for c in range(2)
        ]
        pair = lax.ppermute(pair, ("dom", "col"), far_pairs)
        relayed = lax.ppermute(pair, "col", swapped)
        return received + [side, pair, relayed]

    def exchange_direct(outgoing, k):
        up = [(i, i + 1) for i in range(col - 1)]
        received = [with_partner(outgoing[x], x - 2) for x in direct[::-1]]
        lower = lax.ppermute(outgoing[1], "col", up)
        return received + [lower, lax.ppermute(outgoing[0], "col", [(j, i) for i, j in up])]

    exchange = exchange_relay if relay else exchange_direct

    sent_out = ((send_pad, width), f32)
    vector_out = ((rows, width), f32)
    extended = [pltpu.VMEM((LANE, LANE), f32)]

    place = jnp.full((1, LANE), lax.axis_index("col"), i32)
    (place,) = run(begin_body, [((1, LANE), i32)], (place,), cost=(1_000_000_000, 40_000_000))
    send_ones, sent, *outgoing = run(
        functools.partial(first_body, face, order),
        [((send_pad, rows), bf16), sent_out] + piece_outs,
        (place, send_rows, start_vector),
        cost=(100_000_000_000, 1_000_000_000),
        scratch=[pltpu.VMEM((SUB, LANE), i32)],
    )
    vectors = [start_vector]
    packet = []

    def sums(packet):
        k = len(vectors) - 1
        args = (*vectors, sketch, *packet)
        return run(functools.partial(sums_body, k), [((SUB, LANE), f32)], args, (4_000_000, 2_000_000))

    rest = None
    for k in range(powers):
        final = k + 1 == powers
        received = exchange(outgoing, k)
        if k:
            (vector,) = run(functools.partial(rest_body, k - 1), [vector_out], rest, (1_000_000, 1_000_000))
            vectors.append(vector)
        if k == 0:
            own, *base, neighbour_hot, wide, send_hot, send_wide, shift = run(
                functools.partial(setup_body, face, moves),
                [
                    vector_out,
                    sent_out,
                    ((neighbours * rows, 2 * LANE), bf16),
                    ((neighbours, rows, width), f32),
                    ((neighbours * send_pad, 2 * LANE), bf16),
                    ((neighbours, send_pad, width), f32),
                    ((powers, SUB, LANE), f32),
                ],
                (
                    columns.T,
                    couplings.transpose(1, 0, 2),
                    shifts.reshape(1, powers),
                    place,
                    blocks,
                    start_vector,
                    send_ones,
                    sent,
                ),
                cost=(20_000_000, 4_000_000),
                scratch=[pltpu.VMEM((SUB, LANE), i32)],
            )
        else:
            own, *base = run(
                functools.partial(matvec_body, k),
                [vector_out] if final else [vector_out, sent_out],
                (blocks, vectors[-1], *(() if final else (send_ones, sent, shift))),
                (20_000_000, 4_000_000),
            )
        packet = sums(packet)
        if final:
            vector, packet = run(
                functools.partial(final_body, k, places),
                [vector_out, ((HALF, LANE), f32)],
                (own, neighbour_hot, wide, shift, sketch, *packet, *vectors, *received),
                cost=(4_000_000, 2_000_000),
                scratch=extended,
            )
            vectors.append(vector)
        else:
            keep = k + 2 < powers
            parts, *outgoing = run(
                functools.partial(sends_body, places, keep),
                [((2 * LANE, width), bf16)] + ([sent_out] if keep else []) + piece_outs,
                (*base, vectors[-1], send_hot, send_wide, *received),
                cost=(1_000_000, 1_000_000),
                scratch=extended,
            )
            if keep:
                sent, *outgoing = outgoing
            rest = (own, vectors[-1], neighbour_hot, wide, shift, parts)
    everyone = ("dom", "col")
    packets = lax.all_to_all(jnp.tile(packet, (dom * col, 1)), everyone, 0, 0, tiled=True)
    orthonormal, factor, sketch_factor = run(
        functools.partial(last_body, n, sketches, float(rows * width * dom * col)),
        [((n, rows, width), f32), ((n, n), f32), ((n, n), f32)],
        (packets, *vectors),
        cost=(5_000_000, 1_000_000),
    )
    return orthonormal, factor, sketch_factor


def solution(mesh):
    both = ("dom", "col")
    in_specs = (
        P(both, None, None),
        P(both, None, None),
        P(both, None),
        P(both, None),
        P(),
        P(both, None),
        P(None, both, None),
    )
    out_specs = (P(None, both, None), P(), P())
    return jax.shard_map(shards, mesh=mesh, in_specs=in_specs, out_specs=out_specs, check_vma=False)
```

```python
import functools

import jax
import jax.numpy as jnp
from jax import lax
from jax.experimental import pallas as pl
from jax.experimental.pallas import tpu as pltpu
from jax.sharding import PartitionSpec as P


f32, bf16, i32 = jnp.float32, jnp.bfloat16, jnp.int32
VMEM = pl.BlockSpec(memory_space=pltpu.VMEM)
SUB, LANE = 8, 128
HI_LANE, LO_LANE = 64, 80
HALF, FOLD = 4, 32


def params():
    return pltpu.CompilerParams(vmem_limit_bytes=16 << 20)


def run(body, outs, args, cost=(0, 0), scratch=()):
    return pl.pallas_call(
        body,
        out_shape=[jax.ShapeDtypeStruct(shape, dtype) for shape, dtype in outs],
        in_specs=[VMEM] * len(args),
        out_specs=[VMEM] * len(outs),
        scratch_shapes=list(scratch),
        compiler_params=params(),
        cost_estimate=pl.CostEstimate(flops=cost[0], bytes_accessed=cost[1], transcendentals=0),
    )(*args)


def lanes(shape=(SUB, LANE)):
    return lax.broadcasted_iota(i32, shape, len(shape) - 1)


def subs(shape=(SUB, LANE)):
    return lax.broadcasted_iota(i32, shape, len(shape) - 2)


def two_parts(value):
    high = value.astype(bf16)
    return high, (value - high.astype(f32)).astype(bf16)


def three_parts(value):
    high = value.astype(bf16)
    rest = value - high.astype(f32)
    middle = rest.astype(bf16)
    return high, middle, (rest - middle.astype(f32)).astype(bf16)


def dot(left, right):
    return lax.dot_general(left, right, (((1,), (0,)), ((), ())), preferred_element_type=f32)


def dot_nt(left, right):
    return lax.dot_general(left, right, (((1,), (1,)), ((), ())), preferred_element_type=f32)


def two_sum(a, b):
    total = a + b
    part = total - a
    return total, (a - (total - part)) + (b - part)


def split(a):
    scaled = a * 4097.0
    high = scaled - (scaled - a)
    return high, a - high


def two_product(a, a_split, b_split):
    (ah, al), (bh, bl) = a_split, b_split
    return ah * bh, a * bl + al * bh


def pair_add(a, b):
    total, error = two_sum(a[0], b[0])
    return total, error + (a[1] + b[1])


def take_rows(send_hot, value):
    high, middle, low = three_parts(value)
    return dot(send_hot, high) + dot(send_hot, middle) + dot(send_hot, low)


def write_pieces(picked, out_refs):
    start = 0
    for ref in out_refs:
        ref[...] = picked[start : start + ref.shape[0]]
        start += ref.shape[0]


def one_hot(row, rows):
    wanted = jnp.broadcast_to(row, (LANE, LANE))
    return jnp.where(wanted == subs((LANE, LANE)), 1.0, 0.0).astype(f32).T[:rows]


def begin_body(place_ref, out_ref):
    out_ref[...] = place_ref[...]


def first_body(face, order, place_ref, sends_ref, vector_ref, hot_ref, sent_ref, *rest):
    out_refs, row_ref = rest[:-1], rest[-1]
    row_ref[...] = jnp.full((SUB, LANE), -1, i32)
    even = place_ref[0:1, 0:face] == 0
    for to, (source, odd_source) in enumerate(order):
        taken = sends_ref[:, source * face : (source + 1) * face]
        if odd_source != source:
            taken = jnp.where(even, taken, sends_ref[:, odd_source * face : (odd_source + 1) * face])
        row_ref[0:1, to * face : (to + 1) * face] = taken
    hot = one_hot(row_ref[0:1, :], hot_ref.shape[0])[:, : hot_ref.shape[1]].astype(bf16)
    hot_ref[...] = hot
    sent = take_rows(hot, vector_ref[...])
    sent_ref[...] = sent
    write_pieces(sent, out_refs)


def prepare(face, moves, columns_ref, couplings_ref, place_ref, row_ref, hot_ref, wide_ref):
    neighbours, own_rows = columns_ref.shape
    row_ref[...] = jnp.full((SUB, LANE), -1, i32)
    row_ref[0:neighbours, 0:own_rows] = columns_ref[...]
    columns = row_ref[...]
    even = jnp.broadcast_to(place_ref[...], (SUB, LANE)) == 0
    moved = columns
    for source, targets in enumerate(moves):
        if targets == (source, source):
            continue
        first = own_rows + source * face
        to = [-1 if target is None else columns + (target - source) * face for target in targets]
        inside = (columns >= first) & (columns < first + face)
        moved = jnp.where(inside, jnp.where(even, to[0], to[1]), moved)
    columns = moved
    for k in range(neighbours):
        hot = one_hot(columns[k : k + 1, :], own_rows).astype(bf16)
        hot_ref[k * own_rows : (k + 1) * own_rows, 0:LANE] = hot
        hot_ref[k * own_rows : (k + 1) * own_rows, LANE : 2 * LANE] = hot
        wide_ref[k] = couplings_ref[k].astype(f32)


def matvec(blocks_ref, vector_ref, own_ref):
    sub = subs()
    for g in range(vector_ref.shape[0] // SUB):
        parts = three_parts(vector_ref[g * SUB : (g + 1) * SUB, :])
        left = jnp.concatenate([part.astype(f32) for part in parts], axis=0).astype(bf16)
        total = None
        for b in range(0, SUB, 2):
            start = (g * SUB + b) * LANE
            out = dot_nt(left, blocks_ref[start : start + 2 * LANE, :])
            both = out[:SUB] + (out[SUB : 2 * SUB] + out[2 * SUB :])
            total = both[:, :LANE] if total is None else jnp.where(sub == b, both[:, :LANE], total)
            total = jnp.where(sub == b + 1, both[:, LANE:], total)
        own_ref[g * SUB : (g + 1) * SUB, :] = total


def statistics(k, vectors, sketch_ref, packet):
    rows = vectors[0].shape[0]
    groups = rows // SUB
    sketches = sketch_ref.shape[0]
    lane, sub = lanes(), subs()
    newest = [vectors[k][g * SUB : (g + 1) * SUB, :] for g in range(groups)]
    new_split = [split(x) for x in newest]

    sums = []
    for i in range(sketches):
        row = sketch_ref[i].astype(f32)
        parts = [newest[g] * row[g * SUB : (g + 1) * SUB, :] for g in range(groups)]
        while len(parts) > 1:
            parts = [a + b for a, b in zip(parts[::2], parts[1::2])] + parts[len(parts) // 2 * 2 :]
        sums.append(parts[0])
    high, middle, low = three_parts(jnp.concatenate(sums, axis=0))
    ones = jnp.ones((LANE, LANE), bf16)
    across = dot(high, ones) + dot(middle, ones) + dot(low, ones)
    picked = [jnp.where(lane == i, across[i * SUB : (i + 1) * SUB, :], 0.0) for i in range(sketches)]
    while len(picked) > 1:
        picked = [a + b for a, b in zip(picked[::2], picked[1::2])] + picked[len(picked) // 2 * 2 :]
    sketch_row = picked[0]
    for step in (4, 2, 1):
        sketch_row = sketch_row + pltpu.roll(sketch_row, step, 0)

    wide = (jnp.zeros((SUB, LANE), f32), jnp.zeros((SUB, LANE), f32))
    for l in range(k + 1):
        terms = []
        for g in range(groups):
            other_split = split(vectors[l][g * SUB : (g + 1) * SUB, :]) if l < k else new_split[g]
            terms.append(two_product(newest[g], new_split[g], other_split))
        while len(terms) > 1:
            terms = [pair_add(a, b) for a, b in zip(terms[::2], terms[1::2])] + terms[len(terms) // 2 * 2 :]
        total = terms[0]
        for step in (4, 2, 1):
            total = pair_add(total, tuple(pltpu.roll(x, step, 0) for x in total))
        wide = tuple(jnp.where(sub == l, t, w) for t, w in zip(total, wide))
    for step in (64, 32, 16, 8, 4, 2, 1):
        wide = pair_add(wide, tuple(pltpu.roll(x, step, 1) for x in wide))
    wide = two_sum(*wide)

    row_k = sub == k
    packet = jnp.where(row_k & (lane < sketches), sketch_row, packet)
    for part, first in zip(wide, (HI_LANE, LO_LANE)):
        packet = jnp.where((lane == first + k) & (sub <= k), part, packet)
        turned = jnp.where(lane == first + sub, part, 0.0)
        for step in (4, 2, 1):
            turned = turned + pltpu.roll(turned, step, 0)
        packet = jnp.where(row_k & (lane >= first) & (lane <= first + k), turned, packet)
    return packet


def setup_body(face, moves, *refs):
    columns_ref, couplings_ref, place_ref, own_ref, send_ref, sent_ref, shifts_ref = refs[:7]
    base_ref, hot_ref, wide_ref, send_hot_ref, send_wide_ref, row_ref = refs[7:]
    base_ref[...] = base_of(0, own_ref, send_ref, sent_ref, shifts_ref)
    prepare(face, moves, columns_ref, couplings_ref, place_ref, row_ref, hot_ref, wide_ref)
    neighbours, rows = columns_ref.shape
    count = send_ref.shape[0]
    for k in range(neighbours):
        picked = dot(send_ref[...], hot_ref[k * rows : (k + 1) * rows, :])
        send_hot_ref[k * count : (k + 1) * count, :] = picked.astype(bf16)
        send_wide_ref[k] = dot(send_ref[...], couplings_ref[k])


def shift_of(shifts_ref, k):
    return shifts_ref[0:1, k : k + 1]


def matvec_body(blocks_ref, vector_ref, own_ref):
    matvec(blocks_ref, vector_ref, own_ref)


def base_of(k, own_ref, send_ref, sent_ref, shifts_ref):
    return take_rows(send_ref[...], own_ref[...]) - shift_of(shifts_ref, k) * sent_ref[...]


def sums_body(k, final, *refs):
    vectors, refs = refs[: k + 1], list(refs[k + 1 :])
    if not final:
        base_refs = [refs.pop(0) for _ in range(4)]
        refs.pop()[...] = base_of(k, *base_refs)
    sketch_ref, refs = refs[0], refs[1:]
    packet = refs[0][...] if k > 1 else jnp.zeros((SUB, LANE), f32)
    for newest in range(k if k > 1 else 0, k + 1):
        packet = statistics(newest, vectors, sketch_ref, packet)
    refs[-1][...] = packet


def extend(places, vector_ref, halo_refs, extended_ref):
    rows = vector_ref.shape[0]
    extended_ref[0:rows, :] = vector_ref[...]
    for (first, count, to), ref in zip(places, halo_refs):
        extended_ref[to : to + count, :] = ref[first : first + count, :]
    end = rows + sum(count for _, count, _ in places)
    if end < LANE:
        extended_ref[end:LANE, :] = jnp.zeros((LANE - end, LANE), f32)
    return jnp.concatenate(two_parts(extended_ref[...]), axis=0)


def coupled(base, hot, wide_ref, parts):
    gathered = dot(hot, parts)
    count = base.shape[0]
    for n in range(wide_ref.shape[0]):
        base = base + wide_ref[n] * gathered[n * count : (n + 1) * count]
    return base


def sends_body(places, keep, *refs):
    base_ref, vector_ref, send_hot_ref, send_wide_ref = refs[:4]
    halo_refs, refs = refs[4 : 4 + len(places)], refs[4 + len(places) :]
    parts_ref, extended_ref, out_refs = refs[0], refs[-1], refs[1:-1]
    parts = extend(places, vector_ref, halo_refs, extended_ref)
    parts_ref[...] = parts
    sent = coupled(base_ref[...], send_hot_ref[...], send_wide_ref, parts)
    if keep:
        out_refs[0][...] = sent
        out_refs = out_refs[1:]
    write_pieces(sent, out_refs)


def rest_body(k, own_ref, vector_ref, hot_ref, wide_ref, shifts_ref, parts_ref, next_ref):
    base = own_ref[...] - shift_of(shifts_ref, k) * vector_ref[...]
    next_ref[...] = coupled(base, hot_ref[...], wide_ref, parts_ref[...])


def final_body(k, places, *refs):
    own_ref, hot_ref, wide_ref, shifts_ref, sketch_ref, packet_ref = refs[:6]
    vectors, refs = refs[6 : 7 + k], refs[7 + k :]
    halo_refs, (next_ref, folded_ref, extended_ref) = refs[: len(places)], refs[len(places) :]
    vector_ref = vectors[-1]
    parts = extend(places, vector_ref, halo_refs, extended_ref)
    base = own_ref[...] - shift_of(shifts_ref, k) * vector_ref[...]
    newest = coupled(base, hot_ref[...], wide_ref, parts)
    next_ref[...] = newest
    packet = statistics(k + 1, [*vectors, newest], sketch_ref, packet_ref[...])
    folded_ref[...] = (packet + pltpu.roll(pltpu.roll(packet, HALF, 0), FOLD, 1))[:HALF]


def splat(value, row, column):
    return jnp.broadcast_to(value[row : row + 1, column : column + 1], (SUB, LANE))


def cholesky(entries, n):
    work = {(i, j): entries[i, j] for i in range(n) for j in range(i, n)}
    upper, reciprocal = {}, []
    for p in range(n):
        root = jnp.sqrt(work[p, p])
        inverse = 1.0 / root
        reciprocal.append(inverse)
        upper[p, p] = root
        for j in range(p + 1, n):
            upper[p, j] = work[p, j] * inverse
        for i in range(p + 1, n):
            for j in range(i, n):
                work[i, j] = work[i, j] - upper[p, i] * upper[p, j]
    return upper, reciprocal


def upper_inverse(upper, reciprocal, n):
    result = {}
    for j in range(n):
        result[j, j] = reciprocal[j]
        for i in range(j - 1, -1, -1):
            total = upper[i, j] * result[j, j]
            for m in range(i + 1, j):
                total = total + upper[i, m] * result[m, j]
            result[i, j] = -(total * reciprocal[i])
    return result


def upper_product(left, right, n):
    result = {}
    for i in range(n):
        for j in range(i, n):
            total = left[i, i] * right[i, j]
            for m in range(i + 1, j + 1):
                total = total + left[i, m] * right[m, j]
            result[i, j] = total
    return result


def laid_out(entries, n):
    lane, sub = lanes(), subs()
    rows = jnp.zeros((SUB, LANE), f32)
    for i in range(n):
        row = jnp.zeros((SUB, LANE), f32)
        for j in range(i, n):
            row = jnp.where(lane == j, entries[i, j], row)
        rows = jnp.where(sub == i, row, rows)
    return rows


def times_pair(pair, factor, factor_split):
    product, error = two_product(pair[0], split(pair[0]), factor_split)
    return product, error + pair[1] * factor


def last_body(n, sketches, total_rows, packets_ref, *refs):
    vector_refs, (orthonormal_ref, factor_ref, sketch_factor_ref) = refs[:n], refs[n:]
    lane, sub = lanes(), subs()
    sums = [(packets_ref[i : i + SUB, :], jnp.zeros((SUB, LANE), f32)) for i in range(0, packets_ref.shape[0], SUB)]
    while len(sums) > 1:
        sums = [pair_add(a, b) for a, b in zip(sums[::2], sums[1::2])] + sums[len(sums) // 2 * 2 :]
    folded = pair_add(sums[0], tuple(pltpu.roll(x, HALF, 0) for x in sums[0]))
    total, error = (jnp.where(sub < HALF, x, pltpu.roll(x, LANE - FOLD, 1)) for x in folded)
    low_parts = pltpu.roll(total + error, LANE - (LO_LANE - HI_LANE), 1)
    gram = two_sum(total, error + low_parts)

    sketched = jnp.where(lane < sketches, total + error, 0.0)
    entries = {}
    for j in range(n):
        products = jnp.sum(sketched * jnp.broadcast_to(sketched[j : j + 1, :], (SUB, LANE)), axis=1, keepdims=True)
        column = jnp.broadcast_to(products, (SUB, LANE))
        for i in range(j + 1):
            entries[i, j] = jnp.broadcast_to(column[i : i + 1, :], (SUB, LANE))
    sketch_upper, sketch_reciprocal = cholesky(entries, n)
    mixing = upper_inverse(sketch_upper, sketch_reciprocal, n)

    half = None
    for k in range(n):
        row = jnp.zeros((SUB, LANE), f32)
        for j in range(k, n):
            row = jnp.where(lane == j, mixing[k, j], row)
        at = HI_LANE + k
        column = tuple(jnp.broadcast_to(x[:, at : at + 1], (SUB, LANE)) for x in gram)
        term = times_pair(column, row, split(row))
        half = term if half is None else pair_add(half, term)
    half = two_sum(*half)
    white = None
    for i in range(n):
        column = jnp.zeros((SUB, LANE), f32)
        for j in range(i, n):
            column = jnp.where(sub == j, mixing[i, j], column)
        row = tuple(jnp.broadcast_to(x[i : i + 1, :], (SUB, LANE)) for x in half)
        term = times_pair(row, column, split(column))
        white = term if white is None else pair_add(white, term)
    white = (white[0] + white[1]) / total_rows
    entries = {(i, j): splat(white, i, j) for i in range(n) for j in range(i, n)}
    gram_upper, gram_reciprocal = cholesky(entries, n)
    weights = upper_product(mixing, upper_inverse(gram_upper, gram_reciprocal, n), n)

    for g in range(vector_refs[0].shape[0] // SUB):
        at = slice(g * SUB, (g + 1) * SUB)
        basis = [ref[at, :] for ref in vector_refs]
        for j in range(n):
            value = basis[0] * weights[0, j]
            for i in range(1, j + 1):
                value = value + basis[i] * weights[i, j]
            orthonormal_ref[j, at, :] = value
    factor_ref[...] = laid_out(upper_product(gram_upper, sketch_upper, n), n)[:n, :n]
    sketch_factor_ref[...] = laid_out(sketch_upper, n)[:n, :n]


def with_relay(col, levels):
    return col == 2 and levels >= 2


def shards(diag_blocks, couplings, columns, send_rows, shifts, start_vector, sketch):
    dom, col = lax.axis_size("dom"), lax.axis_size("col")
    levels = dom.bit_length() - 1
    rows, width = start_vector.shape
    neighbours = couplings.shape[1]
    sends = send_rows.shape[1]
    face = sends // (2 + levels)
    powers = shifts.shape[0]
    shifts = shifts.reshape(1, powers)
    n = powers + 1
    sketches = sketch.shape[0]
    blocks = diag_blocks.reshape(rows * width, width)
    relay = with_relay(col, levels)

    near, far = 2 + levels - 2, 2 + levels - 1
    direct = list(range(2, near)) if relay else list(range(2, 2 + levels))
    if relay:
        sizes = [3, 2] + [1] * len(direct)
        order = [(0, 0), (1, 1), (far, near), (near, far), (near, far)] + [(x, x) for x in direct]
        count = 2 + len(direct)
        moves = [(None, 1), (0, None)] + [(x, x) for x in direct] + [(count, count + 1), (count + 1, count)]
        places = [(0, face, rows + x * face) for x in direct]
        places += [(0, 2 * face, rows), (0, face, rows + count * face), (face, face, rows + (count + 1) * face)]
    else:
        sizes = [1] * (2 + levels)
        order = [(x, x) for x in range(2 + levels)]
        moves = order
        places = [(0, face, rows + x * face) for x in direct[::-1] + [0, 1]]
    piece_outs = [((size * face, width), f32) for size in sizes]
    send_pad = -(-len(order) * face // 16) * 16

    def with_partner(piece, level):
        return lax.ppermute(piece, "dom", [(i, i ^ (1 << level)) for i in range(dom)])

    def exchange_relay(outgoing, k):
        side, pair, *rest = outgoing
        swapped = [(0, 1), (1, 0)]
        side = lax.ppermute(side, "col", swapped)
        received = []
        for x, piece in zip(direct, rest):
            received.append(with_partner(piece, x - 2))
        pair = lax.dynamic_update_slice(pair, side[2 * face :], (face, 0))
        far_pairs = [
            (i * 2 + c, (i ^ (1 << (near - 2 + c))) * 2 + c) for i in range(dom) for c in range(2)
        ]
        pair = lax.ppermute(pair, ("dom", "col"), far_pairs)
        relayed = lax.ppermute(pair, "col", swapped)
        return received + [side, pair, relayed]

    def exchange_direct(outgoing, k):
        up = [(i, i + 1) for i in range(col - 1)]
        received = [with_partner(outgoing[x], x - 2) for x in direct[::-1]]
        lower = lax.ppermute(outgoing[1], "col", up)
        return received + [lower, lax.ppermute(outgoing[0], "col", [(j, i) for i, j in up])]

    exchange = exchange_relay if relay else exchange_direct

    sent_out = ((send_pad, width), f32)
    vector_out = ((rows, width), f32)
    extended = [pltpu.VMEM((LANE, LANE), f32)]

    place = jnp.full((1, LANE), lax.axis_index("col"), i32)
    (place,) = run(begin_body, [((1, LANE), i32)], (place,), cost=(1_000_000_000, 40_000_000))
    send_ones, sent, *outgoing = run(
        functools.partial(first_body, face, order),
        [((send_pad, rows), bf16), sent_out] + piece_outs,
        (place, send_rows, start_vector),
        cost=(100_000_000_000, 1_000_000_000),
        scratch=[pltpu.VMEM((SUB, LANE), i32)],
    )
    vectors = [start_vector]
    packet = []

    def sums(packet, final):
        k = len(vectors) - 1
        args = (*vectors, *(() if final else (own, send_ones, sent, shifts)), sketch, *packet)
        outs = [((SUB, LANE), f32)] + ([] if final else [sent_out])
        return run(functools.partial(sums_body, k, final), outs, args, (4_000_000, 2_000_000))

    rest = None
    for k in range(powers):
        final = k + 1 == powers
        received = exchange(outgoing, k)
        if k:
            (vector,) = run(functools.partial(rest_body, k - 1), [vector_out], rest, (1_000_000, 1_000_000))
            vectors.append(vector)
        (own,) = run(matvec_body, [vector_out], (blocks, vectors[-1]), (20_000_000, 4_000_000))
        if k == 0:
            base, neighbour_hot, wide, send_hot, send_wide = run(
                functools.partial(setup_body, face, moves),
                [
                    sent_out,
                    ((neighbours * rows, 2 * LANE), bf16),
                    ((neighbours, rows, width), f32),
                    ((neighbours * send_pad, 2 * LANE), bf16),
                    ((neighbours, send_pad, width), f32),
                ],
                (columns.T, couplings.transpose(1, 0, 2), place, own, send_ones, sent, shifts),
                cost=(4_000_000, 2_000_000),
                scratch=[pltpu.VMEM((SUB, LANE), i32)],
            )
        else:
            packet, base = sums(packet, final) if not final else (*sums(packet, final), None)
            packet = [packet]
        if final:
            vector, packet = run(
                functools.partial(final_body, k, places),
                [vector_out, ((HALF, LANE), f32)],
                (own, neighbour_hot, wide, shifts, sketch, *packet, *vectors, *received),
                cost=(4_000_000, 2_000_000),
                scratch=extended,
            )
            vectors.append(vector)
        else:
            keep = k + 2 < powers
            parts, *outgoing = run(
                functools.partial(sends_body, places, keep),
                [((2 * LANE, width), bf16)] + ([sent_out] if keep else []) + piece_outs,
                (base, vectors[-1], send_hot, send_wide, *received),
                cost=(1_000_000, 1_000_000),
                scratch=extended,
            )
            if keep:
                sent, *outgoing = outgoing
            rest = (own, vectors[-1], neighbour_hot, wide, shifts, parts)
    everyone = ("dom", "col")
    packets = lax.all_to_all(jnp.tile(packet, (dom * col, 1)), everyone, 0, 0, tiled=True)
    orthonormal, factor, sketch_factor = run(
        functools.partial(last_body, n, sketches, float(rows * width * dom * col)),
        [((n, rows, width), f32), ((n, n), f32), ((n, n), f32)],
        (packets, *vectors),
        cost=(5_000_000, 1_000_000),
    )
    return orthonormal, factor, sketch_factor


def solution(mesh):
    both = ("dom", "col")
    in_specs = (
        P(both, None, None),
        P(both, None, None),
        P(both, None),
        P(both, None),
        P(),
        P(both, None),
        P(None, both, None),
    )
    out_specs = (P(None, both, None), P(), P())
    return jax.shard_map(shards, mesh=mesh, in_specs=in_specs, out_specs=out_specs, check_vma=False)
```

```python
import functools

import jax
import jax.numpy as jnp
from jax import lax
from jax.experimental import pallas as pl
from jax.experimental.pallas import tpu as pltpu
from jax.sharding import PartitionSpec as P


f32, bf16, i32 = jnp.float32, jnp.bfloat16, jnp.int32
VMEM = pl.BlockSpec(memory_space=pltpu.VMEM)
SUB, LANE = 8, 128
HI_LANE, LO_LANE = 64, 80
HALF, FOLD = 4, 32


def params():
    return pltpu.CompilerParams(vmem_limit_bytes=16 << 20)


def run(body, outs, args, cost=(0, 0), scratch=()):
    return pl.pallas_call(
        body,
        out_shape=[jax.ShapeDtypeStruct(shape, dtype) for shape, dtype in outs],
        in_specs=[VMEM] * len(args),
        out_specs=[VMEM] * len(outs),
        scratch_shapes=list(scratch),
        compiler_params=params(),
        cost_estimate=pl.CostEstimate(flops=cost[0], bytes_accessed=cost[1], transcendentals=0),
    )(*args)


def lanes(shape=(SUB, LANE)):
    return lax.broadcasted_iota(i32, shape, len(shape) - 1)


def subs(shape=(SUB, LANE)):
    return lax.broadcasted_iota(i32, shape, len(shape) - 2)


def three_parts(value):
    high = value.astype(bf16)
    rest = value - high.astype(f32)
    middle = rest.astype(bf16)
    return high, middle, (rest - middle.astype(f32)).astype(bf16)


def dot(left, right):
    return lax.dot_general(left, right, (((1,), (0,)), ((), ())), preferred_element_type=f32)


def dot_nt(left, right):
    return lax.dot_general(left, right, (((1,), (1,)), ((), ())), preferred_element_type=f32)


def two_sum(a, b):
    total = a + b
    part = total - a
    return total, (a - (total - part)) + (b - part)


def split(a):
    scaled = a * 4097.0
    high = scaled - (scaled - a)
    return high, a - high


def two_product(a, a_split, b_split):
    (ah, al), (bh, bl) = a_split, b_split
    return ah * bh, a * bl + al * bh


def pair_add(a, b):
    total, error = two_sum(a[0], b[0])
    return total, error + (a[1] + b[1])


def take_rows(send_hot, value):
    high, middle, low = three_parts(value)
    return dot(send_hot, high) + dot(send_hot, middle) + dot(send_hot, low)


def write_pieces(picked, out_refs):
    start = 0
    for ref in out_refs:
        ref[...] = picked[start : start + ref.shape[0]]
        start += ref.shape[0]


def one_hot(row, rows):
    wanted = jnp.broadcast_to(row, (LANE, LANE))
    return jnp.where(wanted == subs((LANE, LANE)), 1.0, 0.0).astype(f32).T[:rows]


def begin_body(place_ref, out_ref):
    out_ref[...] = place_ref[...]


def first_body(face, order, place_ref, sends_ref, vector_ref, hot_ref, sent_ref, *rest):
    out_refs, row_ref = rest[:-1], rest[-1]
    row_ref[...] = jnp.full((SUB, LANE), -1, i32)
    even = place_ref[0:1, 0:face] == 0
    for to, (source, odd_source) in enumerate(order):
        taken = sends_ref[:, source * face : (source + 1) * face]
        if odd_source != source:
            taken = jnp.where(even, taken, sends_ref[:, odd_source * face : (odd_source + 1) * face])
        row_ref[0:1, to * face : (to + 1) * face] = taken
    hot = one_hot(row_ref[0:1, :], hot_ref.shape[0])[:, : hot_ref.shape[1]].astype(bf16)
    hot_ref[...] = hot
    sent = take_rows(hot, vector_ref[...])
    sent_ref[...] = sent
    write_pieces(sent, out_refs)


def prepare(face, moves, columns_ref, couplings_ref, place_ref, row_ref, hot_ref, wide_ref):
    neighbours, own_rows = columns_ref.shape
    row_ref[...] = jnp.full((SUB, LANE), -1, i32)
    row_ref[0:neighbours, 0:own_rows] = columns_ref[...]
    columns = row_ref[...]
    even = jnp.broadcast_to(place_ref[...], (SUB, LANE)) == 0
    moved = columns
    for source, targets in enumerate(moves):
        if targets == (source, source):
            continue
        first = own_rows + source * face
        to = [-1 if target is None else columns + (target - source) * face for target in targets]
        inside = (columns >= first) & (columns < first + face)
        moved = jnp.where(inside, jnp.where(even, to[0], to[1]), moved)
    columns = moved
    for k in range(neighbours):
        hot = one_hot(columns[k : k + 1, :], own_rows).astype(bf16)
        hot_ref[k * own_rows : (k + 1) * own_rows, 0:LANE] = hot
        hot_ref[k * own_rows : (k + 1) * own_rows, LANE : 2 * LANE] = hot
        hot_ref[k * own_rows : (k + 1) * own_rows, 2 * LANE : 3 * LANE] = hot
        wide_ref[k] = couplings_ref[k].astype(f32)


def matvec(blocks_ref, vector_ref, own_ref):
    sub = subs()
    for g in range(vector_ref.shape[0] // SUB):
        parts = three_parts(vector_ref[g * SUB : (g + 1) * SUB, :])
        left = jnp.concatenate([part.astype(f32) for part in parts], axis=0).astype(bf16)
        total = None
        for b in range(0, SUB, 2):
            start = (g * SUB + b) * LANE
            out = dot_nt(left, blocks_ref[start : start + 2 * LANE, :])
            both = out[:SUB] + (out[SUB : 2 * SUB] + out[2 * SUB :])
            total = both[:, :LANE] if total is None else jnp.where(sub == b, both[:, :LANE], total)
            total = jnp.where(sub == b + 1, both[:, LANE:], total)
        own_ref[g * SUB : (g + 1) * SUB, :] = total


def statistics(k, vectors, sketch_ref, packet):
    rows = vectors[0].shape[0]
    groups = rows // SUB
    sketches = sketch_ref.shape[0]
    lane, sub = lanes(), subs()
    newest = [vectors[k][g * SUB : (g + 1) * SUB, :] for g in range(groups)]
    new_split = [split(x) for x in newest]

    sums = []
    for i in range(sketches):
        row = sketch_ref[i].astype(f32)
        parts = [newest[g] * row[g * SUB : (g + 1) * SUB, :] for g in range(groups)]
        while len(parts) > 1:
            parts = [a + b for a, b in zip(parts[::2], parts[1::2])] + parts[len(parts) // 2 * 2 :]
        sums.append(parts[0])
    high, middle, low = three_parts(jnp.concatenate(sums, axis=0))
    ones = jnp.ones((LANE, LANE), bf16)
    across = dot(high, ones) + dot(middle, ones) + dot(low, ones)
    picked = [jnp.where(lane == i, across[i * SUB : (i + 1) * SUB, :], 0.0) for i in range(sketches)]
    while len(picked) > 1:
        picked = [a + b for a, b in zip(picked[::2], picked[1::2])] + picked[len(picked) // 2 * 2 :]
    sketch_row = picked[0]
    for step in (4, 2, 1):
        sketch_row = sketch_row + pltpu.roll(sketch_row, step, 0)

    wide = (jnp.zeros((SUB, LANE), f32), jnp.zeros((SUB, LANE), f32))
    for l in range(k + 1):
        terms = []
        for g in range(groups):
            other_split = split(vectors[l][g * SUB : (g + 1) * SUB, :]) if l < k else new_split[g]
            terms.append(two_product(newest[g], new_split[g], other_split))
        while len(terms) > 1:
            terms = [pair_add(a, b) for a, b in zip(terms[::2], terms[1::2])] + terms[len(terms) // 2 * 2 :]
        total = terms[0]
        for step in (4, 2, 1):
            total = pair_add(total, tuple(pltpu.roll(x, step, 0) for x in total))
        wide = tuple(jnp.where(sub == l, t, w) for t, w in zip(total, wide))
    for step in (64, 32, 16, 8, 4, 2, 1):
        wide = pair_add(wide, tuple(pltpu.roll(x, step, 1) for x in wide))
    wide = two_sum(*wide)

    row_k = sub == k
    packet = jnp.where(row_k & (lane < sketches), sketch_row, packet)
    for part, first in zip(wide, (HI_LANE, LO_LANE)):
        packet = jnp.where((lane == first + k) & (sub <= k), part, packet)
        turned = jnp.where(lane == first + sub, part, 0.0)
        for step in (4, 2, 1):
            turned = turned + pltpu.roll(turned, step, 0)
        packet = jnp.where(row_k & (lane >= first) & (lane <= first + k), turned, packet)
    return packet


def setup_body(face, moves, *refs):
    columns_ref, couplings_ref, place_ref, own_ref, send_ref, sent_ref, shifts_ref = refs[:7]
    base_ref, hot_ref, wide_ref, send_hot_ref, send_wide_ref, row_ref = refs[7:]
    base_ref[...] = base_of(0, own_ref, send_ref, sent_ref, shifts_ref)
    prepare(face, moves, columns_ref, couplings_ref, place_ref, row_ref, hot_ref, wide_ref)
    neighbours, rows = columns_ref.shape
    count = send_ref.shape[0]
    for k in range(neighbours):
        picked = dot(send_ref[...], hot_ref[k * rows : (k + 1) * rows, :])
        send_hot_ref[k * count : (k + 1) * count, :] = picked.astype(bf16)
        send_wide_ref[k] = dot(send_ref[...], couplings_ref[k])


def shift_of(shifts_ref, k):
    return shifts_ref[0:1, k : k + 1]


def matvec_body(blocks_ref, vector_ref, own_ref):
    matvec(blocks_ref, vector_ref, own_ref)


def base_of(k, own_ref, send_ref, sent_ref, shifts_ref):
    return take_rows(send_ref[...], own_ref[...]) - shift_of(shifts_ref, k) * sent_ref[...]


def sums_body(k, final, *refs):
    vectors, refs = refs[: k + 1], list(refs[k + 1 :])
    if not final:
        base_refs = [refs.pop(0) for _ in range(4)]
        refs.pop()[...] = base_of(k, *base_refs)
    sketch_ref, refs = refs[0], refs[1:]
    packet = refs[0][...] if k > 1 else jnp.zeros((SUB, LANE), f32)
    for newest in range(k if k > 1 else 0, k + 1):
        packet = statistics(newest, vectors, sketch_ref, packet)
    refs[-1][...] = packet


def extend(places, vector_ref, halo_refs, extended_ref):
    rows = vector_ref.shape[0]
    extended_ref[0:rows, :] = vector_ref[...]
    for (first, count, to), ref in zip(places, halo_refs):
        extended_ref[to : to + count, :] = ref[first : first + count, :]
    end = rows + sum(count for _, count, _ in places)
    if end < LANE:
        extended_ref[end:LANE, :] = jnp.zeros((LANE - end, LANE), f32)
    return jnp.concatenate(three_parts(extended_ref[...]), axis=0)


def coupled(base, hot, wide_ref, parts):
    gathered = dot(hot, parts)
    count = base.shape[0]
    for n in range(wide_ref.shape[0]):
        base = base + wide_ref[n] * gathered[n * count : (n + 1) * count]
    return base


def sends_body(places, keep, *refs):
    base_ref, vector_ref, send_hot_ref, send_wide_ref = refs[:4]
    halo_refs, refs = refs[4 : 4 + len(places)], refs[4 + len(places) :]
    parts_ref, extended_ref, out_refs = refs[0], refs[-1], refs[1:-1]
    parts = extend(places, vector_ref, halo_refs, extended_ref)
    parts_ref[...] = parts
    sent = coupled(base_ref[...], send_hot_ref[...], send_wide_ref, parts)
    if keep:
        out_refs[0][...] = sent
        out_refs = out_refs[1:]
    write_pieces(sent, out_refs)


def rest_body(k, own_ref, vector_ref, hot_ref, wide_ref, shifts_ref, parts_ref, next_ref):
    base = own_ref[...] - shift_of(shifts_ref, k) * vector_ref[...]
    next_ref[...] = coupled(base, hot_ref[...], wide_ref, parts_ref[...])


def final_body(k, places, *refs):
    own_ref, hot_ref, wide_ref, shifts_ref, sketch_ref, packet_ref = refs[:6]
    vectors, refs = refs[6 : 7 + k], refs[7 + k :]
    halo_refs, (next_ref, folded_ref, extended_ref) = refs[: len(places)], refs[len(places) :]
    vector_ref = vectors[-1]
    parts = extend(places, vector_ref, halo_refs, extended_ref)
    base = own_ref[...] - shift_of(shifts_ref, k) * vector_ref[...]
    newest = coupled(base, hot_ref[...], wide_ref, parts)
    next_ref[...] = newest
    packet = statistics(k + 1, [*vectors, newest], sketch_ref, packet_ref[...])
    folded_ref[...] = (packet + pltpu.roll(pltpu.roll(packet, HALF, 0), FOLD, 1))[:HALF]


def splat(value, row, column):
    return jnp.broadcast_to(value[row : row + 1, column : column + 1], (SUB, LANE))


def cholesky(entries, n):
    work = {(i, j): entries[i, j] for i in range(n) for j in range(i, n)}
    upper, reciprocal = {}, []
    for p in range(n):
        root = jnp.sqrt(work[p, p])
        inverse = 1.0 / root
        reciprocal.append(inverse)
        upper[p, p] = root
        for j in range(p + 1, n):
            upper[p, j] = work[p, j] * inverse
        for i in range(p + 1, n):
            for j in range(i, n):
                work[i, j] = work[i, j] - upper[p, i] * upper[p, j]
    return upper, reciprocal


def upper_inverse(upper, reciprocal, n):
    result = {}
    for j in range(n):
        result[j, j] = reciprocal[j]
        for i in range(j - 1, -1, -1):
            total = upper[i, j] * result[j, j]
            for m in range(i + 1, j):
                total = total + upper[i, m] * result[m, j]
            result[i, j] = -(total * reciprocal[i])
    return result


def upper_product(left, right, n):
    result = {}
    for i in range(n):
        for j in range(i, n):
            total = left[i, i] * right[i, j]
            for m in range(i + 1, j + 1):
                total = total + left[i, m] * right[m, j]
            result[i, j] = total
    return result


def laid_out(entries, n):
    lane, sub = lanes(), subs()
    rows = jnp.zeros((SUB, LANE), f32)
    for i in range(n):
        row = jnp.zeros((SUB, LANE), f32)
        for j in range(i, n):
            row = jnp.where(lane == j, entries[i, j], row)
        rows = jnp.where(sub == i, row, rows)
    return rows


def times_pair(pair, factor, factor_split):
    product, error = two_product(pair[0], split(pair[0]), factor_split)
    return product, error + pair[1] * factor


def last_body(n, sketches, total_rows, packets_ref, *refs):
    vector_refs, (orthonormal_ref, factor_ref, sketch_factor_ref) = refs[:n], refs[n:]
    lane, sub = lanes(), subs()
    sums = [(packets_ref[i : i + SUB, :], jnp.zeros((SUB, LANE), f32)) for i in range(0, packets_ref.shape[0], SUB)]
    while len(sums) > 1:
        sums = [pair_add(a, b) for a, b in zip(sums[::2], sums[1::2])] + sums[len(sums) // 2 * 2 :]
    folded = pair_add(sums[0], tuple(pltpu.roll(x, HALF, 0) for x in sums[0]))
    total, error = (jnp.where(sub < HALF, x, pltpu.roll(x, LANE - FOLD, 1)) for x in folded)
    low_parts = pltpu.roll(total + error, LANE - (LO_LANE - HI_LANE), 1)
    gram = two_sum(total, error + low_parts)

    sketched = jnp.where(lane < sketches, total + error, 0.0)
    entries = {}
    for j in range(n):
        products = jnp.sum(sketched * jnp.broadcast_to(sketched[j : j + 1, :], (SUB, LANE)), axis=1, keepdims=True)
        column = jnp.broadcast_to(products, (SUB, LANE))
        for i in range(j + 1):
            entries[i, j] = jnp.broadcast_to(column[i : i + 1, :], (SUB, LANE))
    sketch_upper, sketch_reciprocal = cholesky(entries, n)
    mixing = upper_inverse(sketch_upper, sketch_reciprocal, n)

    half = None
    for k in range(n):
        row = jnp.zeros((SUB, LANE), f32)
        for j in range(k, n):
            row = jnp.where(lane == j, mixing[k, j], row)
        at = HI_LANE + k
        column = tuple(jnp.broadcast_to(x[:, at : at + 1], (SUB, LANE)) for x in gram)
        term = times_pair(column, row, split(row))
        half = term if half is None else pair_add(half, term)
    half = two_sum(*half)
    white = None
    for i in range(n):
        column = jnp.zeros((SUB, LANE), f32)
        for j in range(i, n):
            column = jnp.where(sub == j, mixing[i, j], column)
        row = tuple(jnp.broadcast_to(x[i : i + 1, :], (SUB, LANE)) for x in half)
        term = times_pair(row, column, split(column))
        white = term if white is None else pair_add(white, term)
    white = (white[0] + white[1]) / total_rows
    entries = {(i, j): splat(white, i, j) for i in range(n) for j in range(i, n)}
    gram_upper, gram_reciprocal = cholesky(entries, n)
    weights = upper_product(mixing, upper_inverse(gram_upper, gram_reciprocal, n), n)

    for g in range(vector_refs[0].shape[0] // SUB):
        at = slice(g * SUB, (g + 1) * SUB)
        basis = [ref[at, :] for ref in vector_refs]
        for j in range(n):
            value = basis[0] * weights[0, j]
            for i in range(1, j + 1):
                value = value + basis[i] * weights[i, j]
            orthonormal_ref[j, at, :] = value
    factor_ref[...] = laid_out(upper_product(gram_upper, sketch_upper, n), n)[:n, :n]
    sketch_factor_ref[...] = laid_out(sketch_upper, n)[:n, :n]


def with_relay(col, levels):
    return col == 2 and levels >= 2


def shards(diag_blocks, couplings, columns, send_rows, shifts, start_vector, sketch):
    dom, col = lax.axis_size("dom"), lax.axis_size("col")
    levels = dom.bit_length() - 1
    rows, width = start_vector.shape
    neighbours = couplings.shape[1]
    sends = send_rows.shape[1]
    face = sends // (2 + levels)
    powers = shifts.shape[0]
    shifts = shifts.reshape(1, powers)
    n = powers + 1
    sketches = sketch.shape[0]
    blocks = diag_blocks.reshape(rows * width, width)
    relay = with_relay(col, levels)

    near, far = 2 + levels - 2, 2 + levels - 1
    direct = list(range(2, near)) if relay else list(range(2, 2 + levels))
    if relay:
        sizes = [3, 2] + [1] * len(direct)
        order = [(0, 0), (1, 1), (far, near), (near, far), (near, far)] + [(x, x) for x in direct]
        count = 2 + len(direct)
        moves = [(None, 1), (0, None)] + [(x, x) for x in direct] + [(count, count + 1), (count + 1, count)]
        places = [(0, face, rows + x * face) for x in direct]
        places += [(0, 2 * face, rows), (0, face, rows + count * face), (face, face, rows + (count + 1) * face)]
    else:
        sizes = [1] * (2 + levels)
        order = [(x, x) for x in range(2 + levels)]
        moves = order
        places = [(0, face, rows + x * face) for x in direct[::-1] + [0, 1]]
    piece_outs = [((size * face, width), f32) for size in sizes]
    send_pad = -(-len(order) * face // 16) * 16

    def with_partner(piece, level):
        return lax.ppermute(piece, "dom", [(i, i ^ (1 << level)) for i in range(dom)])

    def exchange_relay(outgoing, k):
        side, pair, *rest = outgoing
        swapped = [(0, 1), (1, 0)]
        side = lax.ppermute(side, "col", swapped)
        received = []
        for x, piece in zip(direct, rest):
            received.append(with_partner(piece, x - 2))
        pair = lax.dynamic_update_slice(pair, side[2 * face :], (face, 0))
        far_pairs = [
            (i * 2 + c, (i ^ (1 << (near - 2 + c))) * 2 + c) for i in range(dom) for c in range(2)
        ]
        pair = lax.ppermute(pair, ("dom", "col"), far_pairs)
        relayed = lax.ppermute(pair, "col", swapped)
        return received + [side, pair, relayed]

    def exchange_direct(outgoing, k):
        up = [(i, i + 1) for i in range(col - 1)]
        received = [with_partner(outgoing[x], x - 2) for x in direct[::-1]]
        lower = lax.ppermute(outgoing[1], "col", up)
        return received + [lower, lax.ppermute(outgoing[0], "col", [(j, i) for i, j in up])]

    exchange = exchange_relay if relay else exchange_direct

    sent_out = ((send_pad, width), f32)
    vector_out = ((rows, width), f32)
    extended = [pltpu.VMEM((LANE, LANE), f32)]

    place = jnp.full((1, LANE), lax.axis_index("col"), i32)
    (place,) = run(begin_body, [((1, LANE), i32)], (place,), cost=(1_000_000_000, 40_000_000))
    send_ones, sent, *outgoing = run(
        functools.partial(first_body, face, order),
        [((send_pad, rows), bf16), sent_out] + piece_outs,
        (place, send_rows, start_vector),
        cost=(100_000_000_000, 1_000_000_000),
        scratch=[pltpu.VMEM((SUB, LANE), i32)],
    )
    vectors = [start_vector]
    packet = []

    def sums(packet, final):
        k = len(vectors) - 1
        args = (*vectors, *(() if final else (own, send_ones, sent, shifts)), sketch, *packet)
        outs = [((SUB, LANE), f32)] + ([] if final else [sent_out])
        return run(functools.partial(sums_body, k, final), outs, args, (4_000_000, 2_000_000))

    rest = None
    for k in range(powers):
        final = k + 1 == powers
        received = exchange(outgoing, k)
        if k:
            (vector,) = run(functools.partial(rest_body, k - 1), [vector_out], rest, (1_000_000, 1_000_000))
            vectors.append(vector)
        (own,) = run(matvec_body, [vector_out], (blocks, vectors[-1]), (20_000_000, 4_000_000))
        if k == 0:
            base, neighbour_hot, wide, send_hot, send_wide = run(
                functools.partial(setup_body, face, moves),
                [
                    sent_out,
                    ((neighbours * rows, 3 * LANE), bf16),
                    ((neighbours, rows, width), f32),
                    ((neighbours * send_pad, 3 * LANE), bf16),
                    ((neighbours, send_pad, width), f32),
                ],
                (columns.T, couplings.transpose(1, 0, 2), place, own, send_ones, sent, shifts),
                cost=(4_000_000, 2_000_000),
                scratch=[pltpu.VMEM((SUB, LANE), i32)],
            )
        else:
            packet, base = sums(packet, final) if not final else (*sums(packet, final), None)
            packet = [packet]
        if final:
            vector, packet = run(
                functools.partial(final_body, k, places),
                [vector_out, ((HALF, LANE), f32)],
                (own, neighbour_hot, wide, shifts, sketch, *packet, *vectors, *received),
                cost=(4_000_000, 2_000_000),
                scratch=extended,
            )
            vectors.append(vector)
        else:
            keep = k + 2 < powers
            parts, *outgoing = run(
                functools.partial(sends_body, places, keep),
                [((3 * LANE, width), bf16)] + ([sent_out] if keep else []) + piece_outs,
                (base, vectors[-1], send_hot, send_wide, *received),
                cost=(1_000_000, 1_000_000),
                scratch=extended,
            )
            if keep:
                sent, *outgoing = outgoing
            rest = (own, vectors[-1], neighbour_hot, wide, shifts, parts)
    everyone = ("dom", "col")
    packets = lax.all_to_all(jnp.tile(packet, (dom * col, 1)), everyone, 0, 0, tiled=True)
    orthonormal, factor, sketch_factor = run(
        functools.partial(last_body, n, sketches, float(rows * width * dom * col)),
        [((n, rows, width), f32), ((n, n), f32), ((n, n), f32)],
        (packets, *vectors),
        cost=(5_000_000, 1_000_000),
    )
    return orthonormal, factor, sketch_factor


def solution(mesh):
    both = ("dom", "col")
    in_specs = (
        P(both, None, None),
        P(both, None, None),
        P(both, None),
        P(both, None),
        P(),
        P(both, None),
        P(None, both, None),
    )
    out_specs = (P(None, both, None), P(), P())
    return jax.shard_map(shards, mesh=mesh, in_specs=in_specs, out_specs=out_specs, check_vma=False)
```
